32 devices in a mesh: zone: 4 (over y, x), slab: 8 (over z, core).
Axes of the slice: x: 2, y: 2, z: 4, core: 2. Of those that a mesh axis runs over, the one named last changes fastest.
Arguments:
- tracers: float32 [4, 4, 2048, 2048], P('zone', None, 'slab'), may hold values from -6 to 6
- velocity: float32 [4, 2, 2048, 2048], P('zone', None, 'slab'), may hold values from -0.2 to 0.2
- diffusivity: float32 [4], replicated, may hold values from 0.02 to 0.12
- owner_dev: int32 [512, 2], P('slab'), may hold values from 0 to 23, all different within a row; in each aligned block of 64 rows (0 to 63, 64 to 127, ...) at most 7 rows name the same one
- owner_seg: int32 [512, 2], P('slab'), may hold values from 0 to 63
- intersection: float32 [512, 2], P('slab'), may hold values from 0.2 to 1
Outputs:
- updated: float32 [4, 4, 2048, 2048], P('zone', None, 'slab')
The draws below stay inside these ranges and needn't reach their ends.
Inputs may be any that keep to these rules, and one draw needn't show every extreme that they name: owner_dev names workpiece slab zone * 8 + slab; the 2 entries of a row differ; the rows of one pin slab name one workpiece slab at most 7 times, and some name one exactly 7 times.
All inputs are finite; a program needn't handle non-finite values.
Results may differ from the reference program's by a relative error of at most 0.00007.
Values sent between devices are 32-bit elements; how exact they have to be, the bound alone decides.
No kernel may reach another device: no remote copies, remote signals or barrier semaphores. Data moves between devices by JAX's collectives and lax.ppermute only.
A program may use at most 128 MiB of HBM per device.

```python
import math
import jax
import jax.numpy as jnp
import numpy as np
from jax import lax

TRACERS = 4
ROWS = 256
COLS = 2048
SEG = 32
INTERSECTIONS = 2
ZONES = 4
NROWS = 2048
SEGS = 64
PIN_SEGS = 512
OWNERS = 24
CAP = 7
N_ZONE = 4
N_SLAB = 8


def with_ends(values, rng, smallest, top_value):
    extent = values.shape
    place = [jax.random.randint(jax.random.fold_in(rng, axis), (), 0, extent[axis]) for axis in range(len(extent))]
    values = values.at[tuple(place)].set(smallest)
    longest = extent.index(max(extent))
    place[longest] = (place[longest] + 1) % extent[longest]
    return values.at[tuple(place)].set(top_value)


def level_of(key, extent, shards, smallest, high):
    def one(dim, blocks):
        draws = jax.random.uniform(jax.random.fold_in(jax.random.fold_in(key, 6), dim), (blocks,), jnp.float32, smallest / len(shards), high / len(shards))
        return jnp.repeat(jnp.exp(draws), extent[dim] // blocks).reshape((-1,) + (1,) * (len(extent) - dim - 1))

    gain = one(*shards[0])
    for cut in shards[1:]:
        gain = gain * one(*cut)
    return gain


def routed_block(own_key, own, number, rows, count, top, limit, skew):
    sequence = jax.random.permutation(own_key, count)
    crowded, usual = portions_of(count, rows * top, limit, skew, True), portions_of(count, rows * top, limit, skew, False)
    places = jnp.arange(count)

    def named(tallies, rotation):
        used = int((tallies > 0).sum())
        fixed = max(1, used // 4)
        passed = fixed + (places - fixed + rotation * (used - fixed)) % max(1, count - fixed)
        return jnp.zeros((count,), jnp.int32).at[sequence[jnp.where(places < fixed, places, passed)]].set(jnp.asarray(tallies, jnp.int32))

    tallies = jnp.where(number % 4 == 0, named(crowded, number // 4), named(usual, number - number // 4 - 1))
    mixed = jax.random.permutation(jax.random.fold_in(own, 3), count)
    source_of, sink = mixed[0:count // 2 * 2:2], mixed[1:count // 2 * 2:2]
    room = jnp.minimum(tallies[source_of] - 1, limit - tallies[sink]) // 2
    room = jnp.where((source_of == sequence[0]) | (sink == sequence[0]) | (tallies[sink] == 0), 0, jnp.maximum(room, 0))
    passed = jax.random.randint(jax.random.fold_in(own, 4), (count // 2,), 0, 1 << 20) % (room + 1)
    tallies = tallies.at[source_of].add(-passed).at[sink].add(passed)
    members = jnp.searchsorted(jnp.cumsum(tallies), jnp.arange(rows * top), side="right").astype(jnp.int32)
    table = members.reshape(top, rows).T
    table = table[jax.random.permutation(jax.random.fold_in(own, 1), rows)]
    rotation = jax.random.randint(jax.random.fold_in(own, 2), (rows, 1), 0, top)
    return jnp.take_along_axis(table, (jnp.arange(top)[None, :] + rotation) % top, axis=1)


def portions_of(count, total, reach, skew, full):
    weights = [(1 << 20) // math.isqrt(rank ** skew) + 1 for rank in range(1, count + 1)]
    largest = reach if full else min(reach, max(-(-total // count), total * weights[0] // sum(weights)))
    least = 1 if total - largest >= count - 1 else 0
    given, rest = [largest] + [least] * (count - 1), total - largest - least * (count - 1)
    while rest > 0:
        free = [i for i in range(1, count) if given[i] < largest] or [i for i in range(1, count) if given[i] < reach]
        pool, budget = sum([weights[i] for i in free]), rest
        for i in free:
            addition = min(reach - given[i], max(1, budget * weights[i] // pool), rest)
            given[i] = given[i] + addition
            rest = rest - addition
    return np.array(given)


def gaussian(own_key, dims, scale, bound, cuts=(), kind=jnp.bfloat16):
    array = scale * jax.random.normal(own_key, dims, jnp.float32)
    if cuts:
        array = array * level_of(own_key, dims, cuts, -0.22, 0.18)
    return jnp.clip(array, -bound, bound).astype(kind)


def setup_inputs(seed: int = 0) -> dict:
    splits = jax.random.split(jax.random.key(seed), 7)
    tracers = gaussian(splits[0], (ZONES, TRACERS, NROWS, COLS), 1.0, 6.0, ((0, 4), (2, 8)), jnp.float32)
    velocity = jnp.clip(jax.random.uniform(splits[1], (ZONES, 2, NROWS, COLS), jnp.float32, -0.2, 0.2) * level_of(splits[1], (ZONES, 2, NROWS, COLS), ((0, 4), (2, 8)), -0.4, 0.0), -0.2, 0.2)
    diffusivity = jnp.clip(jnp.exp(jax.random.uniform(splits[2], (TRACERS,), jnp.float32, math.log(0.02), math.log(0.12))), 0.02, 0.12)
    owner_dev_keys = jax.random.split(jax.random.fold_in(splits[3], 1), PIN_SEGS // SEGS)
    owner_dev_turns = jax.random.permutation(jax.random.fold_in(splits[3], 3), PIN_SEGS // SEGS)
    owner_dev = jax.vmap(lambda own, number: routed_block(jax.random.fold_in(splits[3], 2), own, number, SEGS, OWNERS, INTERSECTIONS, CAP, 2))(owner_dev_keys, owner_dev_turns).reshape((PIN_SEGS, INTERSECTIONS))
    owner_seg = with_ends(jax.random.randint(splits[4], (PIN_SEGS, INTERSECTIONS), 0, SEGS), jax.random.fold_in(splits[4], 1), 0, SEGS - 1).astype(jnp.int32)
    intersection = jnp.clip(0.2 + 0.8 * jax.random.uniform(splits[5], (PIN_SEGS, INTERSECTIONS), jnp.float32) ** level_of(splits[5], (PIN_SEGS, INTERSECTIONS), ((0, 8),), -0.2, 0.2), 0.2, 1.0)
    return dict(tracers=tracers, velocity=velocity, diffusivity=diffusivity, owner_dev=owner_dev, owner_seg=owner_seg, intersection=intersection)


COUPLE = 0.5


def advance(field, velocity, diffusivity):
    zero_row = jnp.zeros_like(field[:, :1])
    upper_row = jnp.concatenate([zero_row, field[:, :-1]], axis=1)
    lower_row = jnp.concatenate([field[:, 1:], zero_row], axis=1)
    left_cells = jnp.roll(field, 1, axis=2)
    right_cells = jnp.roll(field, -1, axis=2)
    along_rows = velocity[0][None]
    along_cols = velocity[1][None]
    transport = jnp.maximum(along_rows, 0.0) * (field - upper_row) + jnp.minimum(along_rows, 0.0) * (lower_row - field)
    transport = transport + jnp.maximum(along_cols, 0.0) * (field - left_cells) + jnp.minimum(along_cols, 0.0) * (right_cells - field)
    laplace = upper_row + lower_row + left_cells + right_cells - 4.0 * field
    return field + diffusivity[:, None, None] * laplace - transport


def reference(tracers, velocity, diffusivity, owner_dev, owner_seg, intersection):
    last_rows = tracers[:, :, ROWS - 1::ROWS, :]
    face = last_rows.reshape(N_ZONE, TRACERS, N_SLAB, SEGS, SEG).transpose(0, 2, 3, 1, 4).reshape(N_ZONE, N_SLAB * SEGS, TRACERS * SEG)
    pin_face = face[N_ZONE - 1]
    work_face = face[:N_ZONE - 1].reshape(-1, TRACERS * SEG)
    target = (owner_dev * SEGS + owner_seg).astype(jnp.int32)
    flux = intersection[:, :, None] * (pin_face[:, None, :] - work_face[target])
    inflow = jax.ops.segment_sum(flux.reshape(-1, TRACERS * SEG), target.reshape(-1), num_segments=(N_ZONE - 1) * N_SLAB * SEGS)
    pin_out = jnp.sum(flux, axis=1)
    coupling = jnp.concatenate([COUPLE * inflow.reshape(N_ZONE - 1, N_SLAB * SEGS, TRACERS * SEG), -(COUPLE * pin_out)[None]], axis=0)
    coupling = coupling.reshape(N_ZONE, N_SLAB, SEGS, TRACERS, SEG).transpose(0, 3, 1, 2, 4).reshape(N_ZONE, TRACERS, N_SLAB, COLS)

    def one_zone(inputs):
        field, speeds, extra = inputs
        stepped = advance(field, speeds, diffusivity)
        return stepped.at[:, ROWS - 1::ROWS, :].add(extra)

    return lax.map(one_zone, (tracers, velocity, coupling))
```

```python
import functools

import jax
import jax.numpy as jnp
from jax import lax
from jax.experimental import pallas as pl
from jax.experimental.pallas import tpu as pltpu
from jax.sharding import PartitionSpec as P

SEG = 32
LANES = 128
TILE = 8
COUPLE = 0.5
HIGHEST = lax.Precision.HIGHEST
VMEM = pl.BlockSpec(memory_space=pltpu.VMEM)
SMEM = pl.BlockSpec(memory_space=pltpu.SMEM)
ANY = pl.BlockSpec(memory_space=pl.ANY)


def permuted(segment, blocks):
    quarters = LANES // SEG
    return (segment % quarters) * blocks + segment // quarters


def lane_group(shape):
    return lax.broadcasted_iota(jnp.int32, shape, len(shape) - 1) // SEG


def to_face(rows):
    quarters = LANES // SEG
    out = []
    for u in range(quarters):
        face = None
        for t, row in enumerate(rows):
            moved = row if t == u else pltpu.roll(row, ((t - u) * SEG) % LANES, 1)
            face = moved if face is None else jnp.where(lane_group(row.shape) == t, moved, face)
        out.append(face)
    return out


def from_face(face, tracer_count):
    quarters = LANES // SEG
    blocks = face.shape[0] // quarters
    rows = []
    for t in range(tracer_count):
        row = None
        for u in range(quarters):
            part = face[u * blocks : (u + 1) * blocks]
            moved = part if t == u else pltpu.roll(part, ((u - t) * SEG) % LANES, 1)
            row = moved if row is None else jnp.where(lane_group(part.shape) == u, moved, row)
        rows.append(row)
    return rows


def pack_kernel(top_ref, bottom_ref, dev_ref, seg_ref, weight_ref, out_ref, first_ref, rows_ref):
    tracer_count, _, cols = bottom_ref.shape[1:]
    blocks = cols // LANES
    segs = dev_ref.shape[0]
    for t in range(tracer_count):
        first_ref[t : t + 1, :] = top_ref[0, t, 0:1, :]
        for c in range(blocks):
            rows_ref[t, c : c + 1, :] = bottom_ref[0, t, TILE - 1 : TILE, c * LANES : (c + 1) * LANES]
    face = to_face([rows_ref[t] for t in range(tracer_count)])
    lane = lax.broadcasted_iota(jnp.int32, (segs, LANES), 1)
    row = lax.broadcasted_iota(jnp.int32, (segs, LANES), 0)
    mine = lane % segs == permuted(row, blocks)
    target = dev_ref[...] * segs + permuted(seg_ref[...], blocks)
    target = target.astype(jnp.float32)
    weight = weight_ref[...]
    fanout = target.shape[1]

    def in_lanes(table):
        picked = table[:, 0:1]
        for k in range(1, fanout):
            picked = jnp.where(lane < k * segs, picked, table[:, k : k + 1])
        return jnp.sum(jnp.where(mine, picked, 0.0), axis=0, keepdims=True)

    targets, weights = in_lanes(target), in_lanes(weight)
    index = lax.broadcasted_iota(jnp.int32, (TILE, LANES), 0)
    tables = jnp.where(index == 0, targets, jnp.where(index == 1, weights, 0.0))
    for slab in range(out_ref.shape[0]):
        for u, part in enumerate(face):
            out_ref[slab, u * blocks : (u + 1) * blocks, :] = part
        out_ref[slab, segs : segs + TILE, :] = tables


def middle_kernel(gathered_ref, dev_ref, seg_ref, weight_ref, out_ref):
    slab_count = gathered_ref.shape[0]
    zone_count, segs, _ = out_ref.shape
    fanout = dev_ref.shape[1]
    quarters = LANES // SEG
    blocks = segs // quarters
    zone, slab = lax.axis_index("zone"), lax.axis_index("slab")
    out_ref[...] = jnp.zeros_like(out_ref)

    def reordered(ref):
        return jnp.concatenate([ref[pl.ds(u, blocks, stride=quarters), :] for u in range(quarters)], axis=0)

    weight = reordered(weight_ref)

    @pl.when(zone < zone_count - 1)
    def _():
        target = reordered(dev_ref) * segs + permuted(reordered(seg_ref), blocks)
        slots = lax.broadcasted_iota(jnp.int32, (segs, slab_count * segs), 1) + zone * (slab_count * segs)
        picker = jnp.zeros(slots.shape, jnp.float32)
        for k in range(fanout):
            picker = picker + jnp.where(target[:, k : k + 1] == slots, weight[:, k : k + 1], 0.0)
        faces = jnp.concatenate([gathered_ref[i, :segs, :] for i in range(slab_count)], axis=0)
        out_ref[zone_count - 1] = jnp.dot(picker, faces, precision=HIGHEST, preferred_element_type=jnp.float32)
        own = lax.broadcasted_iota(jnp.int32, (segs, LANES), 0) + (zone * slab_count + slab) * segs
        own = own.astype(jnp.float32)
        total = jnp.zeros((segs, LANES), jnp.float32)
        for i in range(slab_count):
            hit = gathered_ref[i, segs : segs + 1, :] == own
            total = total + jnp.where(hit, gathered_ref[i, segs + 1 : segs + 2, :], 0.0)
        total = jnp.sum(total, axis=1, keepdims=True)
        out_ref[zone] = -total * gathered_ref[slab, :segs, :]

    @pl.when(zone == zone_count - 1)
    def _():
        for z in range(zone_count - 1):
            own = lax.broadcasted_iota(jnp.int32, (segs, fanout * segs), 0) + (z * slab_count + slab) * segs
            own = own.astype(jnp.float32)
            pickers, faces = [], []
            for i in range(slab_count):
                hit = gathered_ref[i, segs : segs + 1, :] == own
                pickers.append(jnp.where(hit, gathered_ref[i, segs + 1 : segs + 2, :], 0.0))
                faces.extend([gathered_ref[i, :segs, :]] * fanout)
            out_ref[z] = jnp.dot(
                jnp.concatenate(pickers, axis=1),
                jnp.concatenate(faces, axis=0),
                precision=HIGHEST,
                preferred_element_type=jnp.float32,
            )
        total = jnp.sum(weight, axis=1, keepdims=True)
        out_ref[zone_count - 1] = -total * gathered_ref[slab, :segs, :]


def stencil_kernel(
    diffusivity_ref, field_ref, speed_ref, out_ref, top_ref, bottom_ref, up_ref, down_ref,
    field, speed, result, field_sem, speed_sem, out_sem,
):
    _, tracer_count, rows, cols = field_ref.shape
    chunks = out_sem.shape[0]
    step = rows // chunks

    def cut(i):
        return pl.ds(i * step, step)

    loads = [pltpu.make_async_copy(field_ref.at[0, :, cut(i), :], field.at[:, cut(i), :], field_sem.at[i]) for i in range(chunks)]
    speeds = [pltpu.make_async_copy(speed_ref.at[0, :, cut(i), :], speed.at[:, cut(i), :], speed_sem.at[i]) for i in range(chunks)]
    stores = []
    for i in range(chunks):
        low, high = i * step, (i + 1) * step
        low, high = (TILE if i == 0 else low), (rows - TILE if i == chunks - 1 else high)
        piece = pl.ds(low, high - low)
        stores.append(pltpu.make_async_copy(result.at[:, piece, :], out_ref.at[0, :, piece, :], out_sem.at[i]))
    for i in range(chunks):
        loads[i].start()
        speeds[i].start()
    index = lax.broadcasted_iota(jnp.int32, (TILE, cols), 0)

    def tile(low, is_first, is_last, put):
        here = pl.ds(low, TILE)
        a, b = speed[0, here, :], speed[1, here, :]
        a_plus, b_plus = jnp.maximum(a, 0.0), jnp.maximum(b, 0.0)
        a_minus, b_minus = a_plus - a, b_plus - b
        rest = 1.0 - ((a_plus + a_minus) + (b_plus + b_minus))
        for t in range(tracer_count):
            d = diffusivity_ref[t]
            center = field[t, here, :]
            upper = pltpu.roll(center, 1, 0)
            lower = pltpu.roll(center, TILE - 1, 0)
            if is_first:
                upper = jnp.where(index == 0, 0.0, upper)
            else:
                upper = jnp.where(index == 0, pltpu.roll(field[t, pl.ds(low - TILE, TILE), :], 1, 0), upper)
            if is_last:
                lower = jnp.where(index == TILE - 1, 0.0, lower)
            else:
                lower = jnp.where(index == TILE - 1, pltpu.roll(field[t, pl.ds(low + TILE, TILE), :], TILE - 1, 0), lower)
            left = pltpu.roll(center, 1, 1)
            right = pltpu.roll(center, cols - 1, 1)
            up, down = a_plus + d, a_minus + d
            if is_first:
                up_ref[t : t + 1, :] = up[0:1, :]
            if is_last:
                down_ref[t : t + 1, :] = down[TILE - 1 : TILE, :]
            put(
                t,
                (rest - 4.0 * d) * center + up * upper + down * lower + (b_plus + d) * left + (b_minus + d) * right,
            )

    def put_top(t, value):
        top_ref[t] = value

    def put_bottom(t, value):
        bottom_ref[t] = value

    loads[0].wait()
    for i in range(chunks):
        if i + 1 < chunks:
            loads[i + 1].wait()
        speeds[i].wait()
        first, last = i * step // TILE, (i + 1) * step // TILE
        if i == 0:
            tile(0, True, False, put_top)
            first += 1
        if i == chunks - 1:
            last -= 1

        def body(r, carry):
            low = pl.multiple_of(r * TILE, TILE)

            def put(t, value):
                result[t, pl.ds(low, TILE), :] = value

            tile(low, False, False, put)
            return carry

        lax.fori_loop(first, last, body, 0)
        if i == chunks - 1:
            tile(rows - TILE, False, True, put_bottom)
        stores[i].start()
    for store in stores:
        store.wait()


def last_kernel(
    received_ref, gathered_ref, below_ref, top_ref, bottom_ref, up_ref, down_ref, partial_ref,
    out_ref, top, bottom, sem,
):
    zone_count, segs, _ = received_ref.shape
    tracer_count, _, cols = top_ref.shape
    rows = out_ref.shape[2]
    blocks = cols // LANES
    slab = lax.axis_index("slab")
    above = gathered_ref[jnp.maximum(slab - 1, 0), :segs, :]
    above = jnp.where(slab > 0, above, jnp.zeros_like(above))
    coupling = received_ref[0]
    for z in range(1, zone_count):
        coupling = coupling + received_ref[z]
    above = from_face(above, tracer_count)
    coupling = from_face(COUPLE * coupling, tracer_count)
    top[...] = top_ref[...]
    bottom[...] = bottom_ref[...]
    for t in range(tracer_count):
        for c in range(blocks):
            here = slice(c * LANES, (c + 1) * LANES)
            top[t, 0:1, here] = top[t, 0:1, here] + up_ref[t : t + 1, here] * above[t][c : c + 1, :]
            bottom[t, TILE - 1 : TILE, here] = (
                bottom[t, TILE - 1 : TILE, here]
                + down_ref[t : t + 1, here] * below_ref[t : t + 1, here]
                + coupling[t][c : c + 1, :]
            )
    first = pltpu.make_async_copy(top, out_ref.at[0, :, pl.ds(0, TILE), :], sem.at[0])
    second = pltpu.make_async_copy(bottom, out_ref.at[0, :, pl.ds(rows - TILE, TILE), :], sem.at[1])
    first.start()
    second.start()
    first.wait()
    second.wait()


def shards(tracers, velocity, diffusivity, owner_dev, owner_seg, intersection):
    zone_count = lax.axis_size("zone")
    slab_count = lax.axis_size("slab")
    _, tracer_count, rows, cols = tracers.shape
    segs = cols // SEG
    f32 = jnp.float32
    edge = (1, tracer_count, TILE, cols)
    tables = [pl.BlockSpec(table.shape, lambda i: (0, 0)) for table in (owner_dev, owner_seg, intersection)]
    payload, first = pl.pallas_call(
        pack_kernel,
        grid=(1,),
        out_shape=(
            jax.ShapeDtypeStruct((slab_count, segs + TILE, LANES), f32),
            jax.ShapeDtypeStruct((tracer_count, cols), f32),
        ),
        in_specs=[
            pl.BlockSpec(edge, lambda i: (0, 0, 0, 0)),
            pl.BlockSpec(edge, lambda i: (0, 0, rows // TILE - 1, 0)),
            *tables,
        ],
        out_specs=(
            pl.BlockSpec((slab_count, segs + TILE, LANES), lambda i: (0, 0, 0)),
            pl.BlockSpec((tracer_count, cols), lambda i: (0, 0)),
        ),
        scratch_shapes=[pltpu.VMEM((tracer_count, cols // LANES, LANES), f32)],
    )(tracers, tracers, owner_dev, owner_seg, intersection)
    below = lax.ppermute(first, "slab", [(i + 1, i) for i in range(slab_count - 1)])
    gathered = lax.all_to_all(payload, "slab", 0, 0, tiled=True)

    chunks = rows // 32
    edge_tile = jax.ShapeDtypeStruct((tracer_count, TILE, cols), f32)
    edge_row = jax.ShapeDtypeStruct((tracer_count, cols), f32)
    partial, top, bottom, up, down = pl.pallas_call(
        stencil_kernel,
        out_shape=(jax.ShapeDtypeStruct(tracers.shape, f32), edge_tile, edge_tile, edge_row, edge_row),
        in_specs=[SMEM, ANY, ANY],
        out_specs=(ANY, VMEM, VMEM, VMEM, VMEM),
        scratch_shapes=[
            pltpu.VMEM((tracer_count, rows, cols), f32),
            pltpu.VMEM((2, rows, cols), f32),
            pltpu.VMEM((tracer_count, rows, cols), f32),
            pltpu.SemaphoreType.DMA((chunks,)),
            pltpu.SemaphoreType.DMA((chunks,)),
            pltpu.SemaphoreType.DMA((chunks,)),
        ],
        compiler_params=pltpu.CompilerParams(vmem_limit_bytes=32 * 2**20),
        cost_estimate=pl.CostEstimate(
            flops=20 * tracers.size, transcendentals=0, bytes_accessed=4 * (2 * tracers.size + velocity.size)
        ),
    )(diffusivity, tracers, velocity)

    gathered, up = lax.optimization_barrier((gathered, up))
    partials = pl.pallas_call(
        middle_kernel,
        out_shape=jax.ShapeDtypeStruct((zone_count, segs, LANES), f32),
        in_specs=[VMEM] * 4,
        out_specs=VMEM,
    )(gathered, owner_dev, owner_seg, intersection)
    received = lax.all_to_all(partials, "zone", 0, 0, tiled=True)
    return pl.pallas_call(
        last_kernel,
        out_shape=jax.ShapeDtypeStruct(tracers.shape, f32),
        in_specs=[VMEM] * 7 + [ANY],
        out_specs=ANY,
        scratch_shapes=[
            pltpu.VMEM((tracer_count, TILE, cols), f32),
            pltpu.VMEM((tracer_count, TILE, cols), f32),
            pltpu.SemaphoreType.DMA((2,)),
        ],
        input_output_aliases={7: 0},
    )(received, gathered, below, top, bottom, up, down, partial)


def solution(mesh):
    placed = (
        P("zone", None, "slab", None),
        P("zone", None, "slab", None),
        P(),
        P("slab", None),
        P("slab", None),
        P("slab", None),
    )
    return jax.shard_map(
        shards, mesh=mesh, in_specs=placed, out_specs=P("zone", None, "slab", None), check_vma=False
    )
```

```python
import functools

import jax
import jax.numpy as jnp
from jax import lax
from jax.experimental import pallas as pl
from jax.experimental.pallas import tpu as pltpu
from jax.sharding import PartitionSpec as P

SEG = 32
LANES = 128
TILE = 8
COUPLE = 0.5
HIGHEST = lax.Precision.HIGHEST
VMEM = pl.BlockSpec(memory_space=pltpu.VMEM)
SMEM = pl.BlockSpec(memory_space=pltpu.SMEM)
ANY = pl.BlockSpec(memory_space=pl.ANY)


def permuted(segment, blocks):
    quarters = LANES // SEG
    return (segment % quarters) * blocks + segment // quarters


def lane_group(shape):
    return lax.broadcasted_iota(jnp.int32, shape, len(shape) - 1) // SEG


def to_face(rows):
    quarters = LANES // SEG
    out = []
    for u in range(quarters):
        face = None
        for t, row in enumerate(rows):
            moved = row if t == u else pltpu.roll(row, ((t - u) * SEG) % LANES, 1)
            face = moved if face is None else jnp.where(lane_group(row.shape) == t, moved, face)
        out.append(face)
    return out


def from_face(face, tracer_count):
    quarters = LANES // SEG
    blocks = face.shape[0] // quarters
    rows = []
    for t in range(tracer_count):
        row = None
        for u in range(quarters):
            part = face[u * blocks : (u + 1) * blocks]
            moved = part if t == u else pltpu.roll(part, ((u - t) * SEG) % LANES, 1)
            row = moved if row is None else jnp.where(lane_group(part.shape) == u, moved, row)
        rows.append(row)
    return rows


def pack_kernel(top_ref, bottom_ref, dev_ref, seg_ref, weight_ref, out_ref, first_ref, own_ref, rows_ref):
    tracer_count, _, cols = bottom_ref.shape[1:]
    blocks = cols // LANES
    fanout, segs = dev_ref.shape
    for t in range(tracer_count):
        first_ref[t : t + 1, :] = top_ref[0, t, 0:1, :]
        for c in range(blocks):
            rows_ref[t, c : c + 1, :] = bottom_ref[0, t, TILE - 1 : TILE, c * LANES : (c + 1) * LANES]
    face = to_face([rows_ref[t] for t in range(tracer_count)])
    lane = lax.broadcasted_iota(jnp.int32, (segs, segs), 1)
    row = lax.broadcasted_iota(jnp.int32, (segs, segs), 0)
    source = lane == (row % blocks) * (LANES // SEG) + row // blocks
    target = (dev_ref[...] * segs + permuted(seg_ref[...], blocks)).astype(jnp.float32)
    index = lax.broadcasted_iota(jnp.int32, (segs, LANES), 1)
    order = lax.broadcasted_iota(jnp.int32, (segs, LANES), 0)

    def columns(table):
        return [jnp.sum(jnp.where(source, table[k : k + 1, :], 0.0), axis=1, keepdims=True) for k in range(fanout)]

    targets, weights = columns(target), columns(weight_ref[...])
    own_ref[...] = jnp.zeros_like(own_ref)
    lines = []
    for k, column in enumerate([*targets, *weights]):
        own_ref[:, k : k + 1] = column
    for table in (targets, weights):
        line = 0.0
        for k, column in enumerate(table):
            line = line + jnp.where(index == k * segs + order, column, 0.0)
        lines.append(jnp.sum(line, axis=0, keepdims=True))
    targets, weights = lines
    index = lax.broadcasted_iota(jnp.int32, (TILE, LANES), 0)
    tables = jnp.where(index == 0, targets, jnp.where(index == 1, weights, 0.0))
    for slab in range(out_ref.shape[0]):
        for u, part in enumerate(face):
            out_ref[slab, u * blocks : (u + 1) * blocks, :] = part
        out_ref[slab, segs : segs + TILE, :] = tables


def middle_kernel(gathered_ref, own_ref, out_ref):
    slab_count = gathered_ref.shape[0]
    zone_count, segs, _ = out_ref.shape
    fanout = LANES // segs
    zone, slab = lax.axis_index("zone"), lax.axis_index("slab")
    out_ref[...] = jnp.zeros_like(out_ref)

    @pl.when(zone < zone_count - 1)
    def _():
        slots = lax.broadcasted_iota(jnp.int32, (segs, slab_count * segs), 1) + zone * (slab_count * segs)
        slots = slots.astype(jnp.float32)
        picker = jnp.zeros(slots.shape, jnp.float32)
        for k in range(fanout):
            target, weight = own_ref[:, k : k + 1], own_ref[:, fanout + k : fanout + k + 1]
            picker = picker + jnp.where(target == slots, weight, 0.0)
        faces = jnp.concatenate([gathered_ref[i, :segs, :] for i in range(slab_count)], axis=0)
        out_ref[zone_count - 1] = jnp.dot(picker, faces, precision=HIGHEST, preferred_element_type=jnp.float32)
        own = lax.broadcasted_iota(jnp.int32, (segs, LANES), 0) + (zone * slab_count + slab) * segs
        own = own.astype(jnp.float32)
        total = jnp.zeros((segs, LANES), jnp.float32)
        for i in range(slab_count):
            hit = gathered_ref[i, segs : segs + 1, :] == own
            total = total + jnp.where(hit, gathered_ref[i, segs + 1 : segs + 2, :], 0.0)
        total = jnp.sum(total, axis=1, keepdims=True)
        out_ref[zone] = -total * gathered_ref[slab, :segs, :]

    @pl.when(zone == zone_count - 1)
    def _():
        for z in range(zone_count - 1):
            own = lax.broadcasted_iota(jnp.int32, (segs, fanout * segs), 0) + (z * slab_count + slab) * segs
            own = own.astype(jnp.float32)
            pickers, faces = [], []
            for i in range(slab_count):
                hit = gathered_ref[i, segs : segs + 1, :] == own
                pickers.append(jnp.where(hit, gathered_ref[i, segs + 1 : segs + 2, :], 0.0))
                faces.extend([gathered_ref[i, :segs, :]] * fanout)
            out_ref[z] = jnp.dot(
                jnp.concatenate(pickers, axis=1),
                jnp.concatenate(faces, axis=0),
                precision=HIGHEST,
                preferred_element_type=jnp.float32,
            )
        total = jnp.sum(own_ref[:, fanout : 2 * fanout], axis=1, keepdims=True)
        out_ref[zone_count - 1] = -total * gathered_ref[slab, :segs, :]


def stencil_kernel(
    diffusivity_ref, field_ref, speed_ref, out_ref, top_ref, bottom_ref, up_ref, down_ref,
    field, speed, result, field_sem, speed_sem, out_sem,
):
    _, tracer_count, rows, cols = field_ref.shape
    chunks = out_sem.shape[0]
    step = rows // chunks

    def cut(i):
        return pl.ds(i * step, step)

    loads = [pltpu.make_async_copy(field_ref.at[0, :, cut(i), :], field.at[:, cut(i), :], field_sem.at[i]) for i in range(chunks)]
    speeds = [pltpu.make_async_copy(speed_ref.at[0, :, cut(i), :], speed.at[:, cut(i), :], speed_sem.at[i]) for i in range(chunks)]
    stores = []
    for i in range(chunks):
        low, high = i * step, (i + 1) * step
        low, high = (TILE if i == 0 else low), (rows - TILE if i == chunks - 1 else high)
        piece = pl.ds(low, high - low)
        stores.append(pltpu.make_async_copy(result.at[:, piece, :], out_ref.at[0, :, piece, :], out_sem.at[i]))
    for i in range(chunks):
        loads[i].start()
        speeds[i].start()
    index = lax.broadcasted_iota(jnp.int32, (TILE, cols), 0)

    def tile(low, is_first, is_last, put):
        here = pl.ds(low, TILE)
        a, b = speed[0, here, :], speed[1, here, :]
        a_plus, b_plus = jnp.maximum(a, 0.0), jnp.maximum(b, 0.0)
        a_minus, b_minus = a_plus - a, b_plus - b
        rest = 1.0 - ((a_plus + a_minus) + (b_plus + b_minus))
        for t in range(tracer_count):
            d = diffusivity_ref[t]
            center = field[t, here, :]
            upper = pltpu.roll(center, 1, 0)
            lower = pltpu.roll(center, TILE - 1, 0)
            if is_first:
                upper = jnp.where(index == 0, 0.0, upper)
            else:
                upper = jnp.where(index == 0, pltpu.roll(field[t, pl.ds(low - TILE, TILE), :], 1, 0), upper)
            if is_last:
                lower = jnp.where(index == TILE - 1, 0.0, lower)
            else:
                lower = jnp.where(index == TILE - 1, pltpu.roll(field[t, pl.ds(low + TILE, TILE), :], TILE - 1, 0), lower)
            left = pltpu.roll(center, 1, 1)
            right = pltpu.roll(center, cols - 1, 1)
            up, down = a_plus + d, a_minus + d
            if is_first:
                up_ref[t : t + 1, :] = up[0:1, :]
            if is_last:
                down_ref[t : t + 1, :] = down[TILE - 1 : TILE, :]
            put(
                t,
                (rest - 4.0 * d) * center + up * upper + down * lower + (b_plus + d) * left + (b_minus + d) * right,
            )

    def put_top(t, value):
        top_ref[t] = value

    def put_bottom(t, value):
        bottom_ref[t] = value

    loads[0].wait()
    for i in range(chunks):
        if i + 1 < chunks:
            loads[i + 1].wait()
        speeds[i].wait()
        first, last = i * step // TILE, (i + 1) * step // TILE
        if i == 0:
            tile(0, True, False, put_top)
            first += 1
        if i == chunks - 1:
            last -= 1

        def body(r, carry):
            low = pl.multiple_of(r * TILE, TILE)

            def put(t, value):
                result[t, pl.ds(low, TILE), :] = value

            tile(low, False, False, put)
            return carry

        lax.fori_loop(first, last, body, 0)
        if i == chunks - 1:
            tile(rows - TILE, False, True, put_bottom)
        stores[i].start()
    for store in stores:
        store.wait()


def last_kernel(
    received_ref, gathered_ref, below_ref, top_ref, bottom_ref, up_ref, down_ref, partial_ref,
    out_ref, top, bottom, sem,
):
    zone_count, segs, _ = received_ref.shape
    tracer_count, _, cols = top_ref.shape
    rows = out_ref.shape[2]
    blocks = cols // LANES
    slab = lax.axis_index("slab")
    above = gathered_ref[jnp.maximum(slab - 1, 0), :segs, :]
    above = jnp.where(slab > 0, above, jnp.zeros_like(above))
    coupling = received_ref[0]
    for z in range(1, zone_count):
        coupling = coupling + received_ref[z]
    above = from_face(above, tracer_count)
    coupling = from_face(COUPLE * coupling, tracer_count)
    top[...] = top_ref[...]
    bottom[...] = bottom_ref[...]
    for t in range(tracer_count):
        for c in range(blocks):
            here = slice(c * LANES, (c + 1) * LANES)
            top[t, 0:1, here] = top[t, 0:1, here] + up_ref[t : t + 1, here] * above[t][c : c + 1, :]
            bottom[t, TILE - 1 : TILE, here] = (
                bottom[t, TILE - 1 : TILE, here]
                + down_ref[t : t + 1, here] * below_ref[t : t + 1, here]
                + coupling[t][c : c + 1, :]
            )
    first = pltpu.make_async_copy(top, out_ref.at[0, :, pl.ds(0, TILE), :], sem.at[0])
    second = pltpu.make_async_copy(bottom, out_ref.at[0, :, pl.ds(rows - TILE, TILE), :], sem.at[1])
    first.start()
    second.start()
    first.wait()
    second.wait()


def shards(tracers, velocity, diffusivity, owner_dev, owner_seg, intersection):
    zone_count = lax.axis_size("zone")
    slab_count = lax.axis_size("slab")
    _, tracer_count, rows, cols = tracers.shape
    segs = cols // SEG
    f32 = jnp.float32
    small = pltpu.CompilerParams(vmem_limit_bytes=8 * 2**20)
    edge = (1, tracer_count, TILE, cols)
    tracers, velocity, owner_dev, owner_seg, intersection = (
        pltpu.with_memory_space_constraint(x, pltpu.HBM)
        for x in (tracers, velocity, owner_dev.T, owner_seg.T, intersection.T)
    )
    tables = [pl.BlockSpec(table.shape, lambda i: (0, 0)) for table in (owner_dev, owner_seg, intersection)]
    payload, first, own = pl.pallas_call(
        pack_kernel,
        grid=(1,),
        out_shape=(
            jax.ShapeDtypeStruct((slab_count, segs + TILE, LANES), f32),
            jax.ShapeDtypeStruct((tracer_count, cols), f32),
            jax.ShapeDtypeStruct((segs, LANES), f32),
        ),
        in_specs=[
            pl.BlockSpec(edge, lambda i: (0, 0, 0, 0)),
            pl.BlockSpec(edge, lambda i: (0, 0, rows // TILE - 1, 0)),
            *tables,
        ],
        out_specs=(
            pl.BlockSpec((slab_count, segs + TILE, LANES), lambda i: (0, 0, 0)),
            pl.BlockSpec((tracer_count, cols), lambda i: (0, 0)),
            pl.BlockSpec((segs, LANES), lambda i: (0, 0)),
        ),
        compiler_params=small,
        scratch_shapes=[pltpu.VMEM((tracer_count, cols // LANES, LANES), f32)],
    )(tracers, tracers, owner_dev, owner_seg, intersection)
    below = lax.ppermute(first, "slab", [(i + 1, i) for i in range(slab_count - 1)])
    gathered = lax.all_to_all(payload, "slab", 0, 0, tiled=True)

    chunks = rows // 32
    edge_tile = jax.ShapeDtypeStruct((tracer_count, TILE, cols), f32)
    edge_row = jax.ShapeDtypeStruct((tracer_count, cols), f32)
    partial, top, bottom, up, down = pl.pallas_call(
        stencil_kernel,
        out_shape=(jax.ShapeDtypeStruct(tracers.shape, f32), edge_tile, edge_tile, edge_row, edge_row),
        in_specs=[SMEM, ANY, ANY],
        out_specs=(ANY, VMEM, VMEM, VMEM, VMEM),
        scratch_shapes=[
            pltpu.VMEM((tracer_count, rows, cols), f32),
            pltpu.VMEM((2, rows, cols), f32),
            pltpu.VMEM((tracer_count, rows, cols), f32),
            pltpu.SemaphoreType.DMA((chunks,)),
            pltpu.SemaphoreType.DMA((chunks,)),
            pltpu.SemaphoreType.DMA((chunks,)),
        ],
        compiler_params=pltpu.CompilerParams(vmem_limit_bytes=32 * 2**20),
        cost_estimate=pl.CostEstimate(
            flops=20 * tracers.size, transcendentals=0, bytes_accessed=4 * (2 * tracers.size + velocity.size)
        ),
    )(diffusivity, tracers, velocity)

    gathered, below, up = lax.optimization_barrier((gathered, below, up))
    partials = pl.pallas_call(
        middle_kernel,
        out_shape=jax.ShapeDtypeStruct((zone_count, segs, LANES), f32),
        in_specs=[VMEM] * 2,
        out_specs=VMEM,
        compiler_params=small,
    )(gathered, own)
    received = lax.all_to_all(partials, "zone", 0, 0, tiled=True)
    return pl.pallas_call(
        last_kernel,
        out_shape=jax.ShapeDtypeStruct(tracers.shape, f32),
        in_specs=[VMEM] * 7 + [ANY],
        out_specs=ANY,
        scratch_shapes=[
            pltpu.VMEM((tracer_count, TILE, cols), f32),
            pltpu.VMEM((tracer_count, TILE, cols), f32),
            pltpu.SemaphoreType.DMA((2,)),
        ],
        compiler_params=small,
        input_output_aliases={7: 0},
    )(received, gathered, below, top, bottom, up, down, partial)


def solution(mesh):
    placed = (
        P("zone", None, "slab", None),
        P("zone", None, "slab", None),
        P(),
        P("slab", None),
        P("slab", None),
        P("slab", None),
    )
    return jax.shard_map(
        shards, mesh=mesh, in_specs=placed, out_specs=P("zone", None, "slab", None), check_vma=False
    )
```

```python
import functools

import jax
import jax.numpy as jnp
from jax import lax
from jax.experimental import pallas as pl
from jax.experimental.pallas import tpu as pltpu
from jax.sharding import PartitionSpec as P

SEG = 32
LANES = 128
TILE = 8
COUPLE = 0.5
GROUP = 32
PIN = 3
UNROLL = 16
PIECES = (2, 5, 5, 7)
HIGHEST = lax.Precision.HIGHEST
VMEM = pl.BlockSpec(memory_space=pltpu.VMEM)
SMEM = pl.BlockSpec(memory_space=pltpu.SMEM)
ANY = pl.BlockSpec(memory_space=pl.ANY)


def permuted(segment, blocks):
    quarters = LANES // SEG
    return (segment % quarters) * blocks + segment // quarters


def lane_group(shape):
    return lax.broadcasted_iota(jnp.int32, shape, len(shape) - 1) // SEG


def to_face(rows):
    quarters = LANES // SEG
    out = []
    for u in range(quarters):
        face = None
        for t, row in enumerate(rows):
            moved = row if t == u else pltpu.roll(row, ((t - u) * SEG) % LANES, 1)
            face = moved if face is None else jnp.where(lane_group(row.shape) == t, moved, face)
        out.append(face)
    return out


def from_face(face, tracer_count):
    quarters = LANES // SEG
    blocks = face.shape[0] // quarters
    rows = []
    for t in range(tracer_count):
        row = None
        for u in range(quarters):
            part = face[u * blocks : (u + 1) * blocks]
            moved = part if t == u else pltpu.roll(part, ((u - t) * SEG) % LANES, 1)
            row = moved if row is None else jnp.where(lane_group(part.shape) == u, moved, row)
        rows.append(row)
    return rows


def pack_kernel(top_ref, bottom_ref, dev_ref, seg_ref, weight_ref, out_ref, own_ref, rows_ref):
    tracer_count, _, cols = bottom_ref.shape[1:]
    blocks = cols // LANES
    fanout, segs = dev_ref.shape
    for start, row, ref in ((0, TILE - 1, bottom_ref), (segs + TILE, 0, top_ref)):
        for t in range(tracer_count):
            for c in range(blocks):
                rows_ref[t, c : c + 1, :] = ref[0, t, row : row + 1, c * LANES : (c + 1) * LANES]
        for u, part in enumerate(to_face([rows_ref[t] for t in range(tracer_count)])):
            out_ref[start + u * blocks : start + (u + 1) * blocks, :] = part
    lane = lax.broadcasted_iota(jnp.int32, (segs, segs), 1)
    row = lax.broadcasted_iota(jnp.int32, (segs, segs), 0)
    source = lane == (row % blocks) * (LANES // SEG) + row // blocks
    target = (dev_ref[...] * segs + permuted(seg_ref[...], blocks)).astype(jnp.float32)
    index = lax.broadcasted_iota(jnp.int32, (segs, LANES), 1)
    order = lax.broadcasted_iota(jnp.int32, (segs, LANES), 0)

    def columns(table):
        return [jnp.sum(jnp.where(source, table[k : k + 1, :], 0.0), axis=1, keepdims=True) for k in range(fanout)]

    targets, weights = columns(target), columns(weight_ref[...])
    own_ref[...] = jnp.zeros_like(own_ref)
    lines = []
    for k, column in enumerate([*targets, *weights]):
        own_ref[:, k : k + 1] = column
    for table in (targets, weights):
        line = 0.0
        for k, column in enumerate(table):
            line = line + jnp.where(index == k * segs + order, column, 0.0)
        lines.append(jnp.sum(line, axis=0, keepdims=True))
    targets, weights = lines
    index = lax.broadcasted_iota(jnp.int32, (TILE, LANES), 0)
    tables = jnp.where(index == 0, targets, jnp.where(index == 1, weights, 0.0))
    out_ref[segs : segs + TILE, :] = tables


def turned(block, stages):
    return sum(bit for k, bit in enumerate(stages) if block >> k & 1)


def merge_kernel(bit, head_ref, sent_ref, received_ref, out_ref):
    segs = (head_ref.shape[0] - TILE) // 2
    size = sent_ref.shape[0] - segs
    out_ref[:size, :] = sent_ref[:size, :]
    out_ref[size : 2 * size, :] = received_ref[:size, :]
    head = head_ref[head_ref.shape[0] - segs :, :]
    passed = received_ref[size:, :]
    out_ref[2 * size :, :] = jnp.where(lax.axis_index("slab") & bit != 0, head, passed)


def middle_kernel(stages, near_ref, far_ref, own_ref, kept_ref, sent_ref):
    _, segs, _ = sent_ref.shape
    stride = segs + TILE
    half = near_ref.shape[0] // stride
    slab_count = 2 * half
    fanout = LANES // segs
    zone, slab = lax.axis_index("zone"), lax.axis_index("slab")
    parts = [(near_ref, i, slab ^ turned(i, stages)) for i in range(half)]
    parts += [(far_ref, i, slab ^ (turned(i, stages) + stages[-1])) for i in range(half)]
    own_face = near_ref[:segs, :]

    def face(ref, i):
        return ref[i * stride : i * stride + segs, :]

    def line(ref, i, k):
        return ref[i * stride + segs + k : i * stride + segs + k + 1, :]

    order = lax.broadcasted_iota(jnp.int32, (segs, LANES), 0)

    def picked(z):
        own = (order + (z * slab_count + slab) * segs).astype(jnp.float32)
        return [
            jnp.where(line(ref, i, 0) == own, line(ref, i, 1), 0.0) for ref, i, _ in parts
        ]

    @pl.when(zone < PIN)
    def _():
        pickers = []
        for _, _, index in parts:
            slots = lax.broadcasted_iota(jnp.int32, (segs, segs), 1) + (zone * slab_count + index) * segs
            slots = slots.astype(jnp.float32)
            picker = jnp.zeros(slots.shape, jnp.float32)
            for k in range(fanout):
                target, weight = own_ref[:, k : k + 1], own_ref[:, fanout + k : fanout + k + 1]
                picker = picker + jnp.where(target == slots, weight, 0.0)
            pickers.append(picker)
        part = jnp.dot(
            jnp.concatenate(pickers, axis=1),
            jnp.concatenate([face(ref, i) for ref, i, _ in parts], axis=0),
            precision=HIGHEST,
            preferred_element_type=jnp.float32,
        )
        sent_ref[0] = part
        sent_ref[1] = jnp.zeros_like(part)
        kept_ref[1] = part
        total = sum(picked(zone))
        kept_ref[0] = -jnp.sum(total, axis=1, keepdims=True) * own_face

    @pl.when(zone == PIN)
    def _():
        faces = jnp.concatenate([face(ref, i) for ref, i, _ in parts for _ in range(fanout)], axis=0)

        def share(z):
            return jnp.dot(
                jnp.concatenate(picked(z), axis=1), faces, precision=HIGHEST, preferred_element_type=jnp.float32
            )

        sent_ref[0] = share(2)
        sent_ref[1] = share(0)
        kept_ref[1] = share(1)
        total = jnp.sum(own_ref[:, fanout : 2 * fanout], axis=1, keepdims=True)
        kept_ref[0] = -total * own_face


def relay_kernel(kept_ref, received_ref, sent_ref):
    zone = lax.axis_index("zone")
    mine = jnp.where(zone == 2, 0.0, kept_ref[1])
    theirs = jnp.where(zone == 1, received_ref[0], jnp.where(zone == 2, received_ref[1], 0.0))
    sent_ref[...] = mine + theirs


def group(low, field, speed, result, diffusivity):
    tracer_count, rows, cols = field.shape
    tiles = GROUP // TILE
    blocks = cols // LANES
    lane = lax.broadcasted_iota(jnp.int32, (TILE, LANES), 1)
    row = lax.broadcasted_iota(jnp.int32, (TILE, LANES), 0)
    is_left, is_right = lane == 0, lane == LANES - 1
    is_top, is_bottom = row == 0, row == TILE - 1
    above = pl.multiple_of(jnp.maximum(low - TILE, 0), TILE)
    below = pl.multiple_of(jnp.minimum(low + GROUP, rows - TILE), TILE)
    has_above = jnp.where(low > 0, 1.0, 0.0)
    has_below = jnp.where(low + GROUP < rows, 1.0, 0.0)

    def cut(block):
        block = jnp.where(block < 0, blocks - 1, jnp.where(block == blocks, 0, block))
        return pl.ds(pl.multiple_of(block * LANES, LANES), LANES)

    def at(tile):
        return pl.ds(pl.multiple_of(low + tile * TILE, TILE), TILE)

    def column(block, carry):
        here = cut(block)
        speeds = []
        for tile in range(tiles):
            a, b = speed[0, at(tile), here], speed[1, at(tile), here]
            a_plus, b_plus = jnp.maximum(a, 0.0), jnp.maximum(b, 0.0)
            a_minus, b_minus = a_plus - a, b_plus - b
            rest = 1.0 - ((a_plus + a_minus) + (b_plus + b_minus))
            speeds.append((a_plus, a_minus, b_plus, b_minus, rest))
        for t in range(tracer_count):
            d = diffusivity[t]
            center = [field[t, pl.ds(above, TILE), here] * has_above]
            center += [field[t, at(tile), here] for tile in range(tiles)]
            center += [field[t, pl.ds(below, TILE), here] * has_below]
            down = [pltpu.roll(x, 1, 0) for x in center[:-1]]
            up = [pltpu.roll(x, TILE - 1, 0) for x in center[1:]]
            for tile in range(tiles):
                a_plus, a_minus, b_plus, b_minus, rest = speeds[tile]
                x = center[tile + 1]
                upper = jnp.where(is_top, down[tile], down[tile + 1])
                lower = jnp.where(is_bottom, up[tile + 1], up[tile])
                left = pltpu.roll(jnp.where(is_right, field[t, at(tile), cut(block - 1)], x), 1, 1)
                right = pltpu.roll(jnp.where(is_left, field[t, at(tile), cut(block + 1)], x), LANES - 1, 1)
                result[t, at(tile), here] = (
                    (rest - 4.0 * d) * x
                    + (a_plus + d) * upper
                    + (a_minus + d) * lower
                    + (b_plus + d) * left
                    + (b_minus + d) * right
                )
        return carry

    lax.fori_loop(0, blocks, column, 0, unroll=UNROLL)


def span(i):
    return pl.ds(pl.multiple_of(i * GROUP, GROUP), GROUP)


def store(result, out_ref, sem, i):
    return pltpu.make_async_copy(result.at[:, span(i), :], out_ref.at[0, :, span(i), :], sem.at[i])


def run_groups(first, last, field, speed, result, diffusivity, out_ref, sem):
    pending = first
    if first > 0:
        pending = first - 1
        store(result, out_ref, sem, pending).start()

    def body(i, carry):
        group(pl.multiple_of(i * GROUP, GROUP), field, speed, result, diffusivity)

        @pl.when(i < last - 1)
        def _():
            store(result, out_ref, sem, i).start()

        return carry

    lax.fori_loop(first, last, body, 0)
    for i in range(pending, last - 1):
        store(result, out_ref, sem, i).wait()


def first_kernel(count, diffusivity_ref, field_ref, speed_ref, result, out_ref, out_sem):
    run_groups(0, count, field_ref.at[0], speed_ref.at[0], result, diffusivity_ref, out_ref, out_sem)


def next_kernel(
    first, last, diffusivity_ref, field, speed, result_in, out_in, result, out_ref, out_sem
):
    del result_in, out_in
    field, speed = field.at[0], speed.at[0]
    run_groups(first, last, field, speed, result, diffusivity_ref, out_ref, out_sem)


def final_kernel(
    first, last, stages, diffusivity_ref, field, speed, result_in, out_in, far_ref, result, out_ref, out_sem
):
    del result_in, out_in
    field, speed = field.at[0], speed.at[0]
    tracer_count, rows, cols = result.shape
    segs = cols // SEG
    slab = lax.axis_index("slab")
    above = jnp.zeros((segs, LANES), jnp.float32)
    stride = segs + TILE
    half = far_ref.shape[0] // stride
    for i in range(half):
        index = slab ^ (turned(i, stages) + stages[-1])
        above = jnp.where(index == slab - 1, far_ref[i * stride : i * stride + segs, :], above)
    below = jnp.where(slab < 2 * half - 1, far_ref[half * stride :, :], 0.0)
    above, below = from_face(above, tracer_count), from_face(below, tracer_count)
    speeds = speed[0, 0:TILE, :][0:1, :]
    up = jnp.maximum(speeds, 0.0)
    for t in range(tracer_count):
        for c in range(cols // LANES):
            here = slice(c * LANES, (c + 1) * LANES)
            result[t, 0:1, here] = result[t, 0:1, here] + (up[:, here] + diffusivity_ref[t]) * above[t][c : c + 1, :]
    top = pltpu.make_async_copy(result.at[:, :TILE, :], out_ref.at[0, :, :TILE, :], out_sem.at[0])
    top.start()
    run_groups(first, last, field, speed, result, diffusivity_ref, out_ref, out_sem)
    speeds = speed[0, rows - TILE : rows, :][TILE - 1 : TILE, :]
    down = jnp.maximum(speeds, 0.0) - speeds
    for t in range(tracer_count):
        for c in range(cols // LANES):
            here = slice(c * LANES, (c + 1) * LANES)
            row = result[t, rows - TILE :, here][TILE - 1 : TILE, :]
            result[t, rows - 1 : rows, here] = row + (down[:, here] + diffusivity_ref[t]) * below[t][c : c + 1, :]
    rest = pl.ds(rows - GROUP, GROUP - TILE)
    tail = pltpu.make_async_copy(result.at[:, rest, :], out_ref.at[0, :, rest, :], out_sem.at[1])
    tail.start()
    top.wait()
    tail.wait()


def last_kernel(kept_ref, first_ref, second_ref, result, partial_ref, out_ref, bottom, sem):
    del partial_ref
    tracer_count, rows, cols = result.shape
    zone = lax.axis_index("zone")
    coupling = kept_ref[0] + jnp.where(zone >= 2, first_ref[0], 0.0) + jnp.where(zone != 2, second_ref[...], 0.0)
    coupling = from_face(COUPLE * coupling, tracer_count)
    bottom[...] = result[:, rows - TILE :, :]
    for t in range(tracer_count):
        for c in range(cols // LANES):
            here = slice(c * LANES, (c + 1) * LANES)
            bottom[t, TILE - 1 : TILE, here] = bottom[t, TILE - 1 : TILE, here] + coupling[t][c : c + 1, :]
    copy = pltpu.make_async_copy(bottom, out_ref.at[0, :, pl.ds(rows - TILE, TILE), :], sem)
    copy.start()
    copy.wait()


def shards(tracers, velocity, diffusivity, owner_dev, owner_seg, intersection):
    zone_count = lax.axis_size("zone")
    slab_count = lax.axis_size("slab")
    _, tracer_count, rows, cols = tracers.shape
    segs = cols // SEG
    f32 = jnp.float32
    small = pltpu.CompilerParams(vmem_limit_bytes=8 * 2**20)
    edge = (1, tracer_count, TILE, cols)
    arguments = tracers, velocity
    tracers, velocity, owner_dev, owner_seg, intersection = (
        pltpu.with_memory_space_constraint(x, pltpu.HBM)
        for x in (tracers, velocity, owner_dev.T, owner_seg.T, intersection.T)
    )
    tables = [pl.BlockSpec(table.shape, lambda i: (0, 0)) for table in (owner_dev, owner_seg, intersection)]
    payload, own = pl.pallas_call(
        pack_kernel,
        grid=(1,),
        out_shape=(
            jax.ShapeDtypeStruct((2 * segs + TILE, LANES), f32),
            jax.ShapeDtypeStruct((segs, LANES), f32),
        ),
        in_specs=[
            pl.BlockSpec(edge, lambda i: (0, 0, 0, 0)),
            pl.BlockSpec(edge, lambda i: (0, 0, rows // TILE - 1, 0)),
            *tables,
        ],
        out_specs=(
            pl.BlockSpec((2 * segs + TILE, LANES), lambda i: (0, 0)),
            pl.BlockSpec((segs, LANES), lambda i: (0, 0)),
        ),
        compiler_params=small,
        scratch_shapes=[pltpu.VMEM((tracer_count, cols // LANES, LANES), f32)],
    )(tracers, tracers, owner_dev, owner_seg, intersection)
    stages = [slab_count >> (k + 1) for k in range(slab_count.bit_length() - 1)]
    groups = rows // GROUP
    field_shape = jax.ShapeDtypeStruct((tracer_count, rows, cols), f32)
    speed_shape = jax.ShapeDtypeStruct((2, rows, cols), f32)
    out_shape = jax.ShapeDtypeStruct(tracers.shape, f32)
    sems = pltpu.SemaphoreType.DMA((groups,))

    def cost(count):
        return pl.CostEstimate(
            flops=20 * tracers.size * count // groups, transcendentals=0, bytes_accessed=20 * rows * cols * count
        )

    def swap(x, axis, bit):
        return lax.ppermute(x, axis, [(i, i ^ bit) for i in range(lax.axis_size(axis))])

    pieces = [p * groups // 8 for p in PIECES]
    field, speed = (pltpu.with_memory_space_constraint(x, pltpu.VMEM) for x in arguments)

    def begin(last, calm):
        return pl.pallas_call(
            functools.partial(first_kernel, last),
            out_shape=(field_shape, out_shape),
            in_specs=[SMEM, VMEM, VMEM],
            out_specs=(VMEM, ANY),
            scratch_shapes=[sems],
            compiler_params=small,
            cost_estimate=cost(last),
        )(calm, field, speed)

    def go_on(first, last, result, out):
        if first == last:
            return result, out
        return pl.pallas_call(
            functools.partial(next_kernel, first, last),
            out_shape=(field_shape, out_shape),
            in_specs=[SMEM, VMEM, VMEM, VMEM, ANY],
            out_specs=(VMEM, ANY),
            scratch_shapes=[sems],
            input_output_aliases={3: 0, 4: 1},
            compiler_params=small,
            cost_estimate=cost(last - first),
        )(diffusivity, field, speed, result, out)

    near, state = payload, None
    for k, bit in enumerate(stages):
        far = swap(near, "slab", bit)
        early = len(stages) - 3
        if k == early:
            state = begin(pieces[0], diffusivity)
        elif k == early + 1:
            state = go_on(pieces[0], pieces[1], *state)
        elif k == early + 2:
            state = go_on(pieces[1], pieces[2], *state)
        if state is not None:
            near, far, *state = lax.optimization_barrier((near, far, *state))
        if k < len(stages) - 1:
            near = pl.pallas_call(
                functools.partial(merge_kernel, stages[k + 1]),
                out_shape=jax.ShapeDtypeStruct((2 * near.shape[0] - segs, LANES), f32),
                in_specs=[VMEM] * 3,
                out_specs=VMEM,
                compiler_params=small,
            )(payload, near, far)
    result, out = state
    kept, sent = pl.pallas_call(
        functools.partial(middle_kernel, stages),
        out_shape=(jax.ShapeDtypeStruct((2, segs, LANES), f32),) * 2,
        in_specs=[VMEM] * 3,
        out_specs=(VMEM, VMEM),
        compiler_params=small,
    )(near, far, own)
    kept, sent, result, out = lax.optimization_barrier((kept, sent, result, out))
    from_x = swap(sent, "zone", 1)
    result, out = go_on(pieces[2], pieces[3], result, out)
    kept, from_x, result, out = lax.optimization_barrier((kept, from_x, result, out))
    relayed = pl.pallas_call(
        relay_kernel,
        out_shape=jax.ShapeDtypeStruct((segs, LANES), f32),
        in_specs=[VMEM] * 2,
        out_specs=VMEM,
        compiler_params=small,
    )(kept, from_x)
    relayed, result, out = lax.optimization_barrier((relayed, result, out))
    from_y = swap(relayed, "zone", 2)
    result, out = pl.pallas_call(
        functools.partial(final_kernel, pieces[3], groups, stages),
        out_shape=(field_shape, out_shape),
        in_specs=[SMEM, VMEM, VMEM, VMEM, ANY, VMEM],
        out_specs=(VMEM, ANY),
        scratch_shapes=[sems],
        input_output_aliases={3: 0, 4: 1},
        compiler_params=small,
        cost_estimate=cost(groups - pieces[3]),
    )(diffusivity, field, speed, result, out, far)
    return pl.pallas_call(
        last_kernel,
        out_shape=out_shape,
        in_specs=[VMEM] * 4 + [ANY],
        out_specs=ANY,
        scratch_shapes=[pltpu.VMEM((tracer_count, TILE, cols), f32), pltpu.SemaphoreType.DMA],
        compiler_params=small,
        input_output_aliases={4: 0},
    )(kept, from_x, from_y, result, out)


def solution(mesh):
    placed = (
        P("zone", None, "slab", None),
        P("zone", None, "slab", None),
        P(),
        P("slab", None),
        P("slab", None),
        P("slab", None),
    )
    return jax.shard_map(
        shards, mesh=mesh, in_specs=placed, out_specs=P("zone", None, "slab", None), check_vma=False
    )
```

```python
import functools

import jax
import jax.numpy as jnp
from jax import lax
from jax.experimental import pallas as pl
from jax.experimental.pallas import tpu as pltpu
from jax.sharding import PartitionSpec as P

SEG = 32
LANES = 128
TILE = 8
COUPLE = 0.5
GROUP = 32
PIN = 3
UNROLL = 16
PIECES = (2, 5, 5, 7)
HIGHEST = lax.Precision.HIGHEST
VMEM = pl.BlockSpec(memory_space=pltpu.VMEM)
SMEM = pl.BlockSpec(memory_space=pltpu.SMEM)
ANY = pl.BlockSpec(memory_space=pl.ANY)


def permuted(segment, blocks):
    quarters = LANES // SEG
    return (segment % quarters) * blocks + segment // quarters


def lane_group(shape):
    return lax.broadcasted_iota(jnp.int32, shape, len(shape) - 1) // SEG


def to_face(rows):
    quarters = LANES // SEG
    out = []
    for u in range(quarters):
        face = None
        for t, row in enumerate(rows):
            moved = row if t == u else pltpu.roll(row, ((t - u) * SEG) % LANES, 1)
            face = moved if face is None else jnp.where(lane_group(row.shape) == t, moved, face)
        out.append(face)
    return out


def from_face(face, tracer_count):
    quarters = LANES // SEG
    blocks = face.shape[0] // quarters
    rows = []
    for t in range(tracer_count):
        row = None
        for u in range(quarters):
            part = face[u * blocks : (u + 1) * blocks]
            moved = part if t == u else pltpu.roll(part, ((u - t) * SEG) % LANES, 1)
            row = moved if row is None else jnp.where(lane_group(part.shape) == u, moved, row)
        rows.append(row)
    return rows


def pack_kernel(top_ref, bottom_ref, dev_ref, seg_ref, weight_ref, out_ref, own_ref, rows_ref):
    tracer_count, _, cols = bottom_ref.shape[1:]
    blocks = cols // LANES
    fanout, segs = dev_ref.shape
    for start, row, ref in ((0, TILE - 1, bottom_ref), (segs + TILE, 0, top_ref)):
        for t in range(tracer_count):
            for c in range(blocks):
                rows_ref[t, c : c + 1, :] = ref[0, t, row : row + 1, c * LANES : (c + 1) * LANES]
        for u, part in enumerate(to_face([rows_ref[t] for t in range(tracer_count)])):
            out_ref[start + u * blocks : start + (u + 1) * blocks, :] = part
    lane = lax.broadcasted_iota(jnp.int32, (segs, segs), 1)
    row = lax.broadcasted_iota(jnp.int32, (segs, segs), 0)
    source = lane == (row % blocks) * (LANES // SEG) + row // blocks
    target = (dev_ref[...] * segs + permuted(seg_ref[...], blocks)).astype(jnp.float32)
    index = lax.broadcasted_iota(jnp.int32, (segs, LANES), 1)
    order = lax.broadcasted_iota(jnp.int32, (segs, LANES), 0)

    def columns(table):
        return [jnp.sum(jnp.where(source, table[k : k + 1, :], 0.0), axis=1, keepdims=True) for k in range(fanout)]

    targets, weights = columns(target), columns(weight_ref[...])
    own_ref[...] = jnp.zeros_like(own_ref)
    lines = []
    for k, column in enumerate([*targets, *weights]):
        own_ref[:, k : k + 1] = column
    for table in (targets, weights):
        line = 0.0
        for k, column in enumerate(table):
            line = line + jnp.where(index == k * segs + order, column, 0.0)
        lines.append(jnp.sum(line, axis=0, keepdims=True))
    targets, weights = lines
    index = lax.broadcasted_iota(jnp.int32, (TILE, LANES), 0)
    tables = jnp.where(index == 0, targets, jnp.where(index == 1, weights, 0.0))
    out_ref[segs : segs + TILE, :] = tables


def turned(block, stages):
    return sum(bit for k, bit in enumerate(stages) if block >> k & 1)


def merge_kernel(bit, head_ref, sent_ref, received_ref, out_ref):
    segs = (head_ref.shape[0] - TILE) // 2
    size = sent_ref.shape[0] - segs
    out_ref[:size, :] = sent_ref[:size, :]
    out_ref[size : 2 * size, :] = received_ref[:size, :]
    head = head_ref[head_ref.shape[0] - segs :, :]
    passed = received_ref[size:, :]
    out_ref[2 * size :, :] = jnp.where(lax.axis_index("slab") & bit != 0, head, passed)


def middle_kernel(stages, near_ref, far_ref, own_ref, kept_ref, sent_ref):
    _, segs, _ = sent_ref.shape
    stride = segs + TILE
    half = near_ref.shape[0] // stride
    slab_count = 2 * half
    fanout = LANES // segs
    zone, slab = lax.axis_index("zone"), lax.axis_index("slab")
    parts = [(near_ref, i, slab ^ turned(i, stages)) for i in range(half)]
    parts += [(far_ref, i, slab ^ (turned(i, stages) + stages[-1])) for i in range(half)]
    own_face = near_ref[:segs, :]

    def face(ref, i):
        return ref[i * stride : i * stride + segs, :]

    def line(ref, i, k):
        return ref[i * stride + segs + k : i * stride + segs + k + 1, :]

    order = lax.broadcasted_iota(jnp.int32, (segs, LANES), 0)

    def picked(z):
        own = (order + (z * slab_count + slab) * segs).astype(jnp.float32)
        return [
            jnp.where(line(ref, i, 0) == own, line(ref, i, 1), 0.0) for ref, i, _ in parts
        ]

    @pl.when(zone < PIN)
    def _():
        pickers = []
        for _, _, index in parts:
            slots = lax.broadcasted_iota(jnp.int32, (segs, segs), 1) + (zone * slab_count + index) * segs
            slots = slots.astype(jnp.float32)
            picker = jnp.zeros(slots.shape, jnp.float32)
            for k in range(fanout):
                target, weight = own_ref[:, k : k + 1], own_ref[:, fanout + k : fanout + k + 1]
                picker = picker + jnp.where(target == slots, weight, 0.0)
            pickers.append(picker)
        part = jnp.dot(
            jnp.concatenate(pickers, axis=1),
            jnp.concatenate([face(ref, i) for ref, i, _ in parts], axis=0),
            precision=HIGHEST,
            preferred_element_type=jnp.float32,
        )
        sent_ref[0] = part
        sent_ref[1] = jnp.zeros_like(part)
        kept_ref[1] = part
        total = sum(picked(zone))
        kept_ref[0] = -jnp.sum(total, axis=1, keepdims=True) * own_face

    @pl.when(zone == PIN)
    def _():
        faces = jnp.concatenate([face(ref, i) for ref, i, _ in parts for _ in range(fanout)], axis=0)

        def share(z):
            return jnp.dot(
                jnp.concatenate(picked(z), axis=1), faces, precision=HIGHEST, preferred_element_type=jnp.float32
            )

        sent_ref[0] = share(2)
        sent_ref[1] = share(0)
        kept_ref[1] = share(1)
        total = jnp.sum(own_ref[:, fanout : 2 * fanout], axis=1, keepdims=True)
        kept_ref[0] = -total * own_face


def relay_kernel(kept_ref, received_ref, sent_ref):
    zone = lax.axis_index("zone")
    mine = jnp.where(zone == 2, 0.0, kept_ref[1])
    theirs = jnp.where(zone == 1, received_ref[0], jnp.where(zone == 2, received_ref[1], 0.0))
    sent_ref[...] = mine + theirs


def group(low, field, speed, result, diffusivity):
    tracer_count, rows, cols = field.shape
    tiles = GROUP // TILE
    blocks = cols // LANES
    lane = lax.broadcasted_iota(jnp.int32, (TILE, LANES), 1)
    row = lax.broadcasted_iota(jnp.int32, (TILE, LANES), 0)
    is_left, is_right = lane == 0, lane == LANES - 1
    is_top, is_bottom = row == 0, row == TILE - 1
    above = pl.multiple_of(jnp.maximum(low - TILE, 0), TILE)
    below = pl.multiple_of(jnp.minimum(low + GROUP, rows - TILE), TILE)
    has_above = jnp.where(low > 0, 1.0, 0.0)
    has_below = jnp.where(low + GROUP < rows, 1.0, 0.0)

    def cut(block):
        block = jnp.where(block < 0, blocks - 1, jnp.where(block == blocks, 0, block))
        return pl.ds(pl.multiple_of(block * LANES, LANES), LANES)

    def at(tile):
        return pl.ds(pl.multiple_of(low + tile * TILE, TILE), TILE)

    def column(block, carry):
        here = cut(block)
        speeds = []
        for tile in range(tiles):
            a, b = speed[0, at(tile), here], speed[1, at(tile), here]
            a_plus, b_plus = jnp.maximum(a, 0.0), jnp.maximum(b, 0.0)
            a_minus, b_minus = a_plus - a, b_plus - b
            rest = 1.0 - ((a_plus + a_minus) + (b_plus + b_minus))
            speeds.append((a_plus, a_minus, b_plus, b_minus, rest))
        for t in range(tracer_count):
            d = diffusivity[t]
            center = [field[t, pl.ds(above, TILE), here] * has_above]
            center += [field[t, at(tile), here] for tile in range(tiles)]
            center += [field[t, pl.ds(below, TILE), here] * has_below]
            down = [pltpu.roll(x, 1, 0) for x in center[:-1]]
            up = [pltpu.roll(x, TILE - 1, 0) for x in center[1:]]
            for tile in range(tiles):
                a_plus, a_minus, b_plus, b_minus, rest = speeds[tile]
                x = center[tile + 1]
                upper = jnp.where(is_top, down[tile], down[tile + 1])
                lower = jnp.where(is_bottom, up[tile + 1], up[tile])
                left = pltpu.roll(jnp.where(is_right, field[t, at(tile), cut(block - 1)], x), 1, 1)
                right = pltpu.roll(jnp.where(is_left, field[t, at(tile), cut(block + 1)], x), LANES - 1, 1)
                result[t, at(tile), here] = (
                    (rest - 4.0 * d) * x
                    + (a_plus + d) * upper
                    + (a_minus + d) * lower
                    + (b_plus + d) * left
                    + (b_minus + d) * right
                )
        return carry

    lax.fori_loop(0, blocks, column, 0, unroll=UNROLL)


def span(i):
    return pl.ds(pl.multiple_of(i * GROUP, GROUP), GROUP)


def store(result, out_ref, sem, i):
    return pltpu.make_async_copy(result.at[:, span(i), :], out_ref.at[0, :, span(i), :], sem.at[i])


def run_groups(first, last, field, speed, result, diffusivity, out_ref, sem):
    pending = first
    if first > 0:
        pending = first - 1
        store(result, out_ref, sem, pending).start()

    def body(i, carry):
        group(pl.multiple_of(i * GROUP, GROUP), field, speed, result, diffusivity)

        @pl.when(i < last - 1)
        def _():
            store(result, out_ref, sem, i).start()

        return carry

    lax.fori_loop(first, last, body, 0)
    for i in range(pending, last - 1):
        store(result, out_ref, sem, i).wait()


def first_kernel(count, diffusivity_ref, field_ref, speed_ref, result, out_ref, out_sem):
    run_groups(0, count, field_ref.at[0], speed_ref.at[0], result, diffusivity_ref, out_ref, out_sem)


def next_kernel(
    first, last, diffusivity_ref, field, speed, result_in, out_in, result, out_ref, out_sem
):
    del result_in, out_in
    field, speed = field.at[0], speed.at[0]
    run_groups(first, last, field, speed, result, diffusivity_ref, out_ref, out_sem)


def final_kernel(
    first, last, stages, diffusivity_ref, field, speed, result_in, out_in, far_ref, result, out_ref, out_sem
):
    del result_in, out_in
    field, speed = field.at[0], speed.at[0]
    tracer_count, rows, cols = result.shape
    segs = cols // SEG
    slab = lax.axis_index("slab")
    above = jnp.zeros((segs, LANES), jnp.float32)
    stride = segs + TILE
    half = far_ref.shape[0] // stride
    for i in range(half):
        index = slab ^ (turned(i, stages) + stages[-1])
        above = jnp.where(index == slab - 1, far_ref[i * stride : i * stride + segs, :], above)
    below = jnp.where(slab < 2 * half - 1, far_ref[half * stride :, :], 0.0)
    above, below = from_face(above, tracer_count), from_face(below, tracer_count)
    speeds = speed[0, 0:TILE, :][0:1, :]
    up = jnp.maximum(speeds, 0.0)
    for t in range(tracer_count):
        for c in range(cols // LANES):
            here = slice(c * LANES, (c + 1) * LANES)
            result[t, 0:1, here] = result[t, 0:1, here] + (up[:, here] + diffusivity_ref[t]) * above[t][c : c + 1, :]
    top = pltpu.make_async_copy(result.at[:, :TILE, :], out_ref.at[0, :, :TILE, :], out_sem.at[0])
    top.start()
    run_groups(first, last, field, speed, result, diffusivity_ref, out_ref, out_sem)
    speeds = speed[0, rows - TILE : rows, :][TILE - 1 : TILE, :]
    down = jnp.maximum(speeds, 0.0) - speeds
    for t in range(tracer_count):
        for c in range(cols // LANES):
            here = slice(c * LANES, (c + 1) * LANES)
            row = result[t, rows - TILE :, here][TILE - 1 : TILE, :]
            result[t, rows - 1 : rows, here] = row + (down[:, here] + diffusivity_ref[t]) * below[t][c : c + 1, :]
    top.wait()


def last_kernel(kept_ref, first_ref, second_ref, result, partial_ref, out_ref, bottom, sem):
    del partial_ref
    tracer_count, rows, cols = result.shape
    rest = pl.ds(rows - GROUP, GROUP - TILE)
    tail = pltpu.make_async_copy(result.at[:, rest, :], out_ref.at[0, :, rest, :], sem.at[1])
    tail.start()
    zone = lax.axis_index("zone")
    coupling = kept_ref[0] + jnp.where(zone >= 2, first_ref[0], 0.0) + jnp.where(zone != 2, second_ref[...], 0.0)
    coupling = from_face(COUPLE * coupling, tracer_count)
    bottom[...] = result[:, rows - TILE :, :]
    for t in range(tracer_count):
        for c in range(cols // LANES):
            here = slice(c * LANES, (c + 1) * LANES)
            bottom[t, TILE - 1 : TILE, here] = bottom[t, TILE - 1 : TILE, here] + coupling[t][c : c + 1, :]
    copy = pltpu.make_async_copy(bottom, out_ref.at[0, :, pl.ds(rows - TILE, TILE), :], sem.at[0])
    copy.start()
    copy.wait()
    tail.wait()


def shards(tracers, velocity, diffusivity, owner_dev, owner_seg, intersection):
    zone_count = lax.axis_size("zone")
    slab_count = lax.axis_size("slab")
    _, tracer_count, rows, cols = tracers.shape
    segs = cols // SEG
    f32 = jnp.float32
    small = pltpu.CompilerParams(vmem_limit_bytes=8 * 2**20)
    edge = (1, tracer_count, TILE, cols)
    arguments = tracers, velocity
    tracers, velocity, owner_dev, owner_seg, intersection = (
        pltpu.with_memory_space_constraint(x, pltpu.HBM)
        for x in (tracers, velocity, owner_dev.T, owner_seg.T, intersection.T)
    )
    tables = [pl.BlockSpec(table.shape, lambda i: (0, 0)) for table in (owner_dev, owner_seg, intersection)]
    payload, own = pl.pallas_call(
        pack_kernel,
        grid=(1,),
        out_shape=(
            jax.ShapeDtypeStruct((2 * segs + TILE, LANES), f32),
            jax.ShapeDtypeStruct((segs, LANES), f32),
        ),
        in_specs=[
            pl.BlockSpec(edge, lambda i: (0, 0, 0, 0)),
            pl.BlockSpec(edge, lambda i: (0, 0, rows // TILE - 1, 0)),
            *tables,
        ],
        out_specs=(
            pl.BlockSpec((2 * segs + TILE, LANES), lambda i: (0, 0)),
            pl.BlockSpec((segs, LANES), lambda i: (0, 0)),
        ),
        compiler_params=small,
        scratch_shapes=[pltpu.VMEM((tracer_count, cols // LANES, LANES), f32)],
    )(tracers, tracers, owner_dev, owner_seg, intersection)
    stages = [slab_count >> (k + 1) for k in range(slab_count.bit_length() - 1)]
    groups = rows // GROUP
    field_shape = jax.ShapeDtypeStruct((tracer_count, rows, cols), f32)
    speed_shape = jax.ShapeDtypeStruct((2, rows, cols), f32)
    out_shape = jax.ShapeDtypeStruct(tracers.shape, f32)
    sems = pltpu.SemaphoreType.DMA((groups,))

    def cost(count):
        return pl.CostEstimate(
            flops=20 * tracers.size * count // groups, transcendentals=0, bytes_accessed=20 * rows * cols * count
        )

    def swap(x, axis, bit):
        return lax.ppermute(x, axis, [(i, i ^ bit) for i in range(lax.axis_size(axis))])

    pieces = [p * groups // 8 for p in PIECES]
    field, speed = (pltpu.with_memory_space_constraint(x, pltpu.VMEM) for x in arguments)

    def begin(last, calm):
        return pl.pallas_call(
            functools.partial(first_kernel, last),
            out_shape=(field_shape, out_shape),
            in_specs=[SMEM, VMEM, VMEM],
            out_specs=(VMEM, ANY),
            scratch_shapes=[sems],
            compiler_params=small,
            cost_estimate=cost(last),
        )(calm, field, speed)

    def go_on(first, last, result, out):
        if first == last:
            return result, out
        return pl.pallas_call(
            functools.partial(next_kernel, first, last),
            out_shape=(field_shape, out_shape),
            in_specs=[SMEM, VMEM, VMEM, VMEM, ANY],
            out_specs=(VMEM, ANY),
            scratch_shapes=[sems],
            input_output_aliases={3: 0, 4: 1},
            compiler_params=small,
            cost_estimate=cost(last - first),
        )(diffusivity, field, speed, result, out)

    near, state = payload, None
    for k, bit in enumerate(stages):
        far = swap(near, "slab", bit)
        early = len(stages) - 3
        if k == early:
            state = begin(pieces[0], diffusivity)
        elif k == early + 1:
            state = go_on(pieces[0], pieces[1], *state)
        elif k == early + 2:
            state = go_on(pieces[1], pieces[2], *state)
        if state is not None:
            near, far, *state = lax.optimization_barrier((near, far, *state))
        if k < len(stages) - 1:
            near = pl.pallas_call(
                functools.partial(merge_kernel, stages[k + 1]),
                out_shape=jax.ShapeDtypeStruct((2 * near.shape[0] - segs, LANES), f32),
                in_specs=[VMEM] * 3,
                out_specs=VMEM,
                compiler_params=small,
            )(payload, near, far)
    result, out = state
    kept, sent = pl.pallas_call(
        functools.partial(middle_kernel, stages),
        out_shape=(jax.ShapeDtypeStruct((2, segs, LANES), f32),) * 2,
        in_specs=[VMEM] * 3,
        out_specs=(VMEM, VMEM),
        compiler_params=small,
    )(near, far, own)
    kept, sent, result, out = lax.optimization_barrier((kept, sent, result, out))
    from_x = swap(sent, "zone", 1)
    result, out = go_on(pieces[2], pieces[3], result, out)
    kept, from_x, result, out = lax.optimization_barrier((kept, from_x, result, out))
    relayed = pl.pallas_call(
        relay_kernel,
        out_shape=jax.ShapeDtypeStruct((segs, LANES), f32),
        in_specs=[VMEM] * 2,
        out_specs=VMEM,
        compiler_params=small,
    )(kept, from_x)
    relayed, result, out = lax.optimization_barrier((relayed, result, out))
    from_y = swap(relayed, "zone", 2)
    result, out = pl.pallas_call(
        functools.partial(final_kernel, pieces[3], groups, stages),
        out_shape=(field_shape, out_shape),
        in_specs=[SMEM, VMEM, VMEM, VMEM, ANY, VMEM],
        out_specs=(VMEM, ANY),
        scratch_shapes=[sems],
        input_output_aliases={3: 0, 4: 1},
        compiler_params=small,
        cost_estimate=cost(groups - pieces[3]),
    )(diffusivity, field, speed, result, out, far)
    return pl.pallas_call(
        last_kernel,
        out_shape=out_shape,
        in_specs=[VMEM] * 4 + [ANY],
        out_specs=ANY,
        scratch_shapes=[pltpu.VMEM((tracer_count, TILE, cols), f32), pltpu.SemaphoreType.DMA((2,))],
        compiler_params=small,
        input_output_aliases={4: 0},
    )(kept, from_x, from_y, result, out)


def solution(mesh):
    placed = (
        P("zone", None, "slab", None),
        P("zone", None, "slab", None),
        P(),
        P("slab", None),
        P("slab", None),
        P("slab", None),
    )
    return jax.shard_map(
        shards, mesh=mesh, in_specs=placed, out_specs=P("zone", None, "slab", None), check_vma=False
    )
```

```python
import functools

import jax
import jax.numpy as jnp
from jax import lax
from jax.experimental import pallas as pl
from jax.experimental.pallas import tpu as pltpu
from jax.sharding import PartitionSpec as P

SEG = 32
LANES = 128
TILE = 8
COUPLE = 0.5
GROUP = 32
PIN = 3
UNROLL = 16
PIECES = (2, 5, 5, 7)
HIGHEST = lax.Precision.HIGHEST
VMEM = pl.BlockSpec(memory_space=pltpu.VMEM)
SMEM = pl.BlockSpec(memory_space=pltpu.SMEM)
ANY = pl.BlockSpec(memory_space=pl.ANY)


def permuted(segment, blocks):
    quarters = LANES // SEG
    return (segment % quarters) * blocks + segment // quarters


def lane_group(shape):
    return lax.broadcasted_iota(jnp.int32, shape, len(shape) - 1) // SEG


def to_face(rows):
    quarters = LANES // SEG
    out = []
    for u in range(quarters):
        face = None
        for t, row in enumerate(rows):
            moved = row if t == u else pltpu.roll(row, ((t - u) * SEG) % LANES, 1)
            face = moved if face is None else jnp.where(lane_group(row.shape) == t, moved, face)
        out.append(face)
    return out


def from_face(face, tracer_count):
    quarters = LANES // SEG
    blocks = face.shape[0] // quarters
    rows = []
    for t in range(tracer_count):
        row = None
        for u in range(quarters):
            part = face[u * blocks : (u + 1) * blocks]
            moved = part if t == u else pltpu.roll(part, ((u - t) * SEG) % LANES, 1)
            row = moved if row is None else jnp.where(lane_group(part.shape) == u, moved, row)
        rows.append(row)
    return rows


def pack_kernel(top_ref, bottom_ref, dev_ref, seg_ref, weight_ref, out_ref, own_ref, rows_ref):
    tracer_count, _, cols = bottom_ref.shape[1:]
    blocks = cols // LANES
    fanout, segs = dev_ref.shape
    for start, row, ref in ((0, TILE - 1, bottom_ref), (segs + TILE, 0, top_ref)):
        for t in range(tracer_count):
            for c in range(blocks):
                rows_ref[t, c : c + 1, :] = ref[0, t, row : row + 1, c * LANES : (c + 1) * LANES]
        for u, part in enumerate(to_face([rows_ref[t] for t in range(tracer_count)])):
            out_ref[start + u * blocks : start + (u + 1) * blocks, :] = part
    lane = lax.broadcasted_iota(jnp.int32, (segs, segs), 1)
    row = lax.broadcasted_iota(jnp.int32, (segs, segs), 0)
    source = lane == (row % blocks) * (LANES // SEG) + row // blocks
    target = (dev_ref[...] * segs + permuted(seg_ref[...], blocks)).astype(jnp.float32)
    index = lax.broadcasted_iota(jnp.int32, (segs, LANES), 1)
    order = lax.broadcasted_iota(jnp.int32, (segs, LANES), 0)

    def columns(table):
        return [jnp.sum(jnp.where(source, table[k : k + 1, :], 0.0), axis=1, keepdims=True) for k in range(fanout)]

    targets, weights = columns(target), columns(weight_ref[...])
    own_ref[...] = jnp.zeros_like(own_ref)
    lines = []
    for k, column in enumerate([*targets, *weights]):
        own_ref[:, k : k + 1] = column
    for table in (targets, weights):
        line = 0.0
        for k, column in enumerate(table):
            line = line + jnp.where(index == k * segs + order, column, 0.0)
        lines.append(jnp.sum(line, axis=0, keepdims=True))
    targets, weights = lines
    index = lax.broadcasted_iota(jnp.int32, (TILE, LANES), 0)
    tables = jnp.where(index == 0, targets, jnp.where(index == 1, weights, 0.0))
    out_ref[segs : segs + TILE, :] = tables


def turned(block, stages):
    return sum(bit for k, bit in enumerate(stages) if block >> k & 1)


def merge_kernel(bit, head_ref, sent_ref, received_ref, out_ref):
    segs = (head_ref.shape[0] - TILE) // 2
    size = sent_ref.shape[0] - segs
    out_ref[:size, :] = sent_ref[:size, :]
    out_ref[size : 2 * size, :] = received_ref[:size, :]
    head = head_ref[head_ref.shape[0] - segs :, :]
    passed = received_ref[size:, :]
    out_ref[2 * size :, :] = jnp.where(lax.axis_index("slab") & bit != 0, head, passed)


def middle_kernel(stages, near_ref, far_ref, own_ref, kept_ref, sent_ref):
    _, segs, _ = sent_ref.shape
    stride = segs + TILE
    half = near_ref.shape[0] // stride
    slab_count = 2 * half
    fanout = LANES // segs
    zone, slab = lax.axis_index("zone"), lax.axis_index("slab")
    parts = [(near_ref, i, slab ^ turned(i, stages)) for i in range(half)]
    parts += [(far_ref, i, slab ^ (turned(i, stages) + stages[-1])) for i in range(half)]
    own_face = near_ref[:segs, :]

    def face(ref, i):
        return ref[i * stride : i * stride + segs, :]

    def line(ref, i, k):
        return ref[i * stride + segs + k : i * stride + segs + k + 1, :]

    order = lax.broadcasted_iota(jnp.int32, (segs, LANES), 0)

    def picked(z):
        own = (order + (z * slab_count + slab) * segs).astype(jnp.float32)
        return [
            jnp.where(line(ref, i, 0) == own, line(ref, i, 1), 0.0) for ref, i, _ in parts
        ]

    @pl.when(zone < PIN)
    def _():
        pickers = []
        for _, _, index in parts:
            slots = lax.broadcasted_iota(jnp.int32, (segs, segs), 1) + (zone * slab_count + index) * segs
            slots = slots.astype(jnp.float32)
            picker = jnp.zeros(slots.shape, jnp.float32)
            for k in range(fanout):
                target, weight = own_ref[:, k : k + 1], own_ref[:, fanout + k : fanout + k + 1]
                picker = picker + jnp.where(target == slots, weight, 0.0)
            pickers.append(picker)
        part = jnp.dot(
            jnp.concatenate(pickers, axis=1),
            jnp.concatenate([face(ref, i) for ref, i, _ in parts], axis=0),
            precision=HIGHEST,
            preferred_element_type=jnp.float32,
        )
        sent_ref[0] = part
        sent_ref[1] = jnp.zeros_like(part)
        kept_ref[1] = part
        total = sum(picked(zone))
        kept_ref[0] = -jnp.sum(total, axis=1, keepdims=True) * own_face

    @pl.when(zone == PIN)
    def _():
        faces = jnp.concatenate([face(ref, i) for ref, i, _ in parts], axis=0)

        lane = lax.broadcasted_iota(jnp.int32, (segs, LANES), 1)

        def columns(z):
            sums = [x + pltpu.roll(x, segs, 1) for x in picked(z)]
            return jnp.concatenate(
                [jnp.where(lane < segs, sums[i], sums[i + 1]) for i in range(0, len(sums), 2)], axis=1
            )

        pickers = jnp.concatenate([columns(z) for z in (2, 0, 1)], axis=0)
        shares = jnp.dot(pickers, faces, precision=HIGHEST, preferred_element_type=jnp.float32)
        sent_ref[0] = shares[:segs]
        sent_ref[1] = shares[segs : 2 * segs]
        kept_ref[1] = shares[2 * segs :]
        total = jnp.sum(own_ref[:, fanout : 2 * fanout], axis=1, keepdims=True)
        kept_ref[0] = -total * own_face


def relay_kernel(kept_ref, received_ref, sent_ref):
    zone = lax.axis_index("zone")
    mine = jnp.where(zone == 2, 0.0, kept_ref[1])
    theirs = jnp.where(zone == 1, received_ref[0], jnp.where(zone == 2, received_ref[1], 0.0))
    sent_ref[...] = mine + theirs


def group(low, field, speed, result, diffusivity):
    tracer_count, rows, cols = field.shape
    tiles = GROUP // TILE
    blocks = cols // LANES
    lane = lax.broadcasted_iota(jnp.int32, (TILE, LANES), 1)
    row = lax.broadcasted_iota(jnp.int32, (TILE, LANES), 0)
    is_left, is_right = lane == 0, lane == LANES - 1
    is_top, is_bottom = row == 0, row == TILE - 1
    above = pl.multiple_of(jnp.maximum(low - TILE, 0), TILE)
    below = pl.multiple_of(jnp.minimum(low + GROUP, rows - TILE), TILE)
    has_above = jnp.where(low > 0, 1.0, 0.0)
    has_below = jnp.where(low + GROUP < rows, 1.0, 0.0)

    def cut(block):
        block = jnp.where(block < 0, blocks - 1, jnp.where(block == blocks, 0, block))
        return pl.ds(pl.multiple_of(block * LANES, LANES), LANES)

    def at(tile):
        return pl.ds(pl.multiple_of(low + tile * TILE, TILE), TILE)

    def column(block, carry):
        here = cut(block)
        speeds = []
        for tile in range(tiles):
            a, b = speed[0, at(tile), here], speed[1, at(tile), here]
            a_plus, b_plus = jnp.maximum(a, 0.0), jnp.maximum(b, 0.0)
            a_minus, b_minus = a_plus - a, b_plus - b
            rest = 1.0 - ((a_plus + a_minus) + (b_plus + b_minus))
            speeds.append((a_plus, a_minus, b_plus, b_minus, rest))
        for t in range(tracer_count):
            d = diffusivity[t]
            center = [field[t, pl.ds(above, TILE), here] * has_above]
            center += [field[t, at(tile), here] for tile in range(tiles)]
            center += [field[t, pl.ds(below, TILE), here] * has_below]
            down = [pltpu.roll(x, 1, 0) for x in center[:-1]]
            up = [pltpu.roll(x, TILE - 1, 0) for x in center[1:]]
            for tile in range(tiles):
                a_plus, a_minus, b_plus, b_minus, rest = speeds[tile]
                x = center[tile + 1]
                upper = jnp.where(is_top, down[tile], down[tile + 1])
                lower = jnp.where(is_bottom, up[tile + 1], up[tile])
                left = pltpu.roll(jnp.where(is_right, field[t, at(tile), cut(block - 1)], x), 1, 1)
                right = pltpu.roll(jnp.where(is_left, field[t, at(tile), cut(block + 1)], x), LANES - 1, 1)
                result[t, at(tile), here] = (
                    (rest - 4.0 * d) * x
                    + (a_plus + d) * upper
                    + (a_minus + d) * lower
                    + (b_plus + d) * left
                    + (b_minus + d) * right
                )
        return carry

    lax.fori_loop(0, blocks, column, 0, unroll=UNROLL)


def span(i):
    return pl.ds(pl.multiple_of(i * GROUP, GROUP), GROUP)


def store(result, out_ref, sem, i):
    return pltpu.make_async_copy(result.at[:, span(i), :], out_ref.at[0, :, span(i), :], sem.at[i])


def run_groups(first, last, field, speed, result, diffusivity, out_ref, sem):
    pending = first
    if first > 0:
        pending = first - 1
        store(result, out_ref, sem, pending).start()

    def body(i, carry):
        group(pl.multiple_of(i * GROUP, GROUP), field, speed, result, diffusivity)

        @pl.when(i < last - 1)
        def _():
            store(result, out_ref, sem, i).start()

        return carry

    lax.fori_loop(first, last, body, 0)
    for i in range(pending, last - 1):
        store(result, out_ref, sem, i).wait()


def first_kernel(count, diffusivity_ref, field_ref, speed_ref, result, out_ref, out_sem):
    run_groups(0, count, field_ref.at[0], speed_ref.at[0], result, diffusivity_ref, out_ref, out_sem)


def next_kernel(
    first, last, diffusivity_ref, field, speed, result_in, out_in, result, out_ref, out_sem
):
    del result_in, out_in
    field, speed = field.at[0], speed.at[0]
    run_groups(first, last, field, speed, result, diffusivity_ref, out_ref, out_sem)


def final_kernel(
    first, last, stages, diffusivity_ref, field, speed, result_in, out_in, far_ref, result, out_ref, out_sem
):
    del result_in, out_in
    field, speed = field.at[0], speed.at[0]
    tracer_count, rows, cols = result.shape
    segs = cols // SEG
    slab = lax.axis_index("slab")
    above = jnp.zeros((segs, LANES), jnp.float32)
    stride = segs + TILE
    half = far_ref.shape[0] // stride
    for i in range(half):
        index = slab ^ (turned(i, stages) + stages[-1])
        above = jnp.where(index == slab - 1, far_ref[i * stride : i * stride + segs, :], above)
    below = jnp.where(slab < 2 * half - 1, far_ref[half * stride :, :], 0.0)
    above, below = from_face(above, tracer_count), from_face(below, tracer_count)
    speeds = speed[0, 0:TILE, :][0:1, :]
    up = jnp.maximum(speeds, 0.0)
    for t in range(tracer_count):
        for c in range(cols // LANES):
            here = slice(c * LANES, (c + 1) * LANES)
            result[t, 0:1, here] = result[t, 0:1, here] + (up[:, here] + diffusivity_ref[t]) * above[t][c : c + 1, :]
    top = pltpu.make_async_copy(result.at[:, :TILE, :], out_ref.at[0, :, :TILE, :], out_sem.at[0])
    top.start()
    run_groups(first, last, field, speed, result, diffusivity_ref, out_ref, out_sem)
    speeds = speed[0, rows - TILE : rows, :][TILE - 1 : TILE, :]
    down = jnp.maximum(speeds, 0.0) - speeds
    for t in range(tracer_count):
        for c in range(cols // LANES):
            here = slice(c * LANES, (c + 1) * LANES)
            row = result[t, rows - TILE :, here][TILE - 1 : TILE, :]
            result[t, rows - 1 : rows, here] = row + (down[:, here] + diffusivity_ref[t]) * below[t][c : c + 1, :]
    top.wait()


def last_kernel(kept_ref, first_ref, second_ref, result, partial_ref, out_ref, bottom, sem):
    del partial_ref
    tracer_count, rows, cols = result.shape
    rest = pl.ds(rows - GROUP, GROUP - TILE)
    tail = pltpu.make_async_copy(result.at[:, rest, :], out_ref.at[0, :, rest, :], sem.at[1])
    tail.start()
    zone = lax.axis_index("zone")
    coupling = kept_ref[0] + jnp.where(zone >= 2, first_ref[0], 0.0) + jnp.where(zone != 2, second_ref[...], 0.0)
    coupling = from_face(COUPLE * coupling, tracer_count)
    bottom[...] = result[:, rows - TILE :, :]
    for t in range(tracer_count):
        for c in range(cols // LANES):
            here = slice(c * LANES, (c + 1) * LANES)
            bottom[t, TILE - 1 : TILE, here] = bottom[t, TILE - 1 : TILE, here] + coupling[t][c : c + 1, :]
    copy = pltpu.make_async_copy(bottom, out_ref.at[0, :, pl.ds(rows - TILE, TILE), :], sem.at[0])
    copy.start()
    copy.wait()
    tail.wait()


def shards(tracers, velocity, diffusivity, owner_dev, owner_seg, intersection):
    zone_count = lax.axis_size("zone")
    slab_count = lax.axis_size("slab")
    _, tracer_count, rows, cols = tracers.shape
    segs = cols // SEG
    f32 = jnp.float32
    small = pltpu.CompilerParams(vmem_limit_bytes=8 * 2**20)
    edge = (1, tracer_count, TILE, cols)
    arguments = tracers, velocity
    tracers, velocity, owner_dev, owner_seg, intersection = (
        pltpu.with_memory_space_constraint(x, pltpu.HBM)
        for x in (tracers, velocity, owner_dev.T, owner_seg.T, intersection.T)
    )
    tables = [pl.BlockSpec(table.shape, lambda i: (0, 0)) for table in (owner_dev, owner_seg, intersection)]
    payload, own = pl.pallas_call(
        pack_kernel,
        grid=(1,),
        out_shape=(
            jax.ShapeDtypeStruct((2 * segs + TILE, LANES), f32),
            jax.ShapeDtypeStruct((segs, LANES), f32),
        ),
        in_specs=[
            pl.BlockSpec(edge, lambda i: (0, 0, 0, 0)),
            pl.BlockSpec(edge, lambda i: (0, 0, rows // TILE - 1, 0)),
            *tables,
        ],
        out_specs=(
            pl.BlockSpec((2 * segs + TILE, LANES), lambda i: (0, 0)),
            pl.BlockSpec((segs, LANES), lambda i: (0, 0)),
        ),
        compiler_params=small,
        scratch_shapes=[pltpu.VMEM((tracer_count, cols // LANES, LANES), f32)],
    )(tracers, tracers, owner_dev, owner_seg, intersection)
    stages = [slab_count >> (k + 1) for k in range(slab_count.bit_length() - 1)]
    groups = rows // GROUP
    field_shape = jax.ShapeDtypeStruct((tracer_count, rows, cols), f32)
    speed_shape = jax.ShapeDtypeStruct((2, rows, cols), f32)
    out_shape = jax.ShapeDtypeStruct(tracers.shape, f32)
    sems = pltpu.SemaphoreType.DMA((groups,))

    def cost(count):
        return pl.CostEstimate(
            flops=20 * tracers.size * count // groups, transcendentals=0, bytes_accessed=20 * rows * cols * count
        )

    def swap(x, axis, bit):
        return lax.ppermute(x, axis, [(i, i ^ bit) for i in range(lax.axis_size(axis))])

    pieces = [p * groups // 8 for p in PIECES]
    field, speed = (pltpu.with_memory_space_constraint(x, pltpu.VMEM) for x in arguments)

    def begin(last, calm):
        return pl.pallas_call(
            functools.partial(first_kernel, last),
            out_shape=(field_shape, out_shape),
            in_specs=[SMEM, VMEM, VMEM],
            out_specs=(VMEM, ANY),
            scratch_shapes=[sems],
            compiler_params=small,
            cost_estimate=cost(last),
        )(calm, field, speed)

    def go_on(first, last, result, out):
        if first == last:
            return result, out
        return pl.pallas_call(
            functools.partial(next_kernel, first, last),
            out_shape=(field_shape, out_shape),
            in_specs=[SMEM, VMEM, VMEM, VMEM, ANY],
            out_specs=(VMEM, ANY),
            scratch_shapes=[sems],
            input_output_aliases={3: 0, 4: 1},
            compiler_params=small,
            cost_estimate=cost(last - first),
        )(diffusivity, field, speed, result, out)

    near, state = payload, None
    for k, bit in enumerate(stages):
        far = swap(near, "slab", bit)
        early = len(stages) - 3
        if k == early:
            state = begin(pieces[0], diffusivity)
        elif k == early + 1:
            state = go_on(pieces[0], pieces[1], *state)
        elif k == early + 2:
            state = go_on(pieces[1], pieces[2], *state)
        if state is not None:
            near, far, *state = lax.optimization_barrier((near, far, *state))
        if k < len(stages) - 1:
            near = pl.pallas_call(
                functools.partial(merge_kernel, stages[k + 1]),
                out_shape=jax.ShapeDtypeStruct((2 * near.shape[0] - segs, LANES), f32),
                in_specs=[VMEM] * 3,
                out_specs=VMEM,
                compiler_params=small,
            )(payload, near, far)
    result, out = state
    kept, sent = pl.pallas_call(
        functools.partial(middle_kernel, stages),
        out_shape=(jax.ShapeDtypeStruct((2, segs, LANES), f32),) * 2,
        in_specs=[VMEM] * 3,
        out_specs=(VMEM, VMEM),
        compiler_params=small,
    )(near, far, own)
    kept, sent, result, out = lax.optimization_barrier((kept, sent, result, out))
    from_x = swap(sent, "zone", 1)
    result, out = go_on(pieces[2], pieces[3], result, out)
    kept, from_x, result, out = lax.optimization_barrier((kept, from_x, result, out))
    relayed = pl.pallas_call(
        relay_kernel,
        out_shape=jax.ShapeDtypeStruct((segs, LANES), f32),
        in_specs=[VMEM] * 2,
        out_specs=VMEM,
        compiler_params=small,
    )(kept, from_x)
    relayed, result, out = lax.optimization_barrier((relayed, result, out))
    from_y = swap(relayed, "zone", 2)
    result, out = pl.pallas_call(
        functools.partial(final_kernel, pieces[3], groups, stages),
        out_shape=(field_shape, out_shape),
        in_specs=[SMEM, VMEM, VMEM, VMEM, ANY, VMEM],
        out_specs=(VMEM, ANY),
        scratch_shapes=[sems],
        input_output_aliases={3: 0, 4: 1},
        compiler_params=small,
        cost_estimate=cost(groups - pieces[3]),
    )(diffusivity, field, speed, result, out, far)
    return pl.pallas_call(
        last_kernel,
        out_shape=out_shape,
        in_specs=[VMEM] * 4 + [ANY],
        out_specs=ANY,
        scratch_shapes=[pltpu.VMEM((tracer_count, TILE, cols), f32), pltpu.SemaphoreType.DMA((2,))],
        compiler_params=small,
        input_output_aliases={4: 0},
    )(kept, from_x, from_y, result, out)


def solution(mesh):
    placed = (
        P("zone", None, "slab", None),
        P("zone", None, "slab", None),
        P(),
        P("slab", None),
        P("slab", None),
        P("slab", None),
    )
    return jax.shard_map(
        shards, mesh=mesh, in_specs=placed, out_specs=P("zone", None, "slab", None), check_vma=False
    )
```
